128 devices in a mesh: dp: 64 (over y_hi, z, x, core), col: 2 (over y_lo).
Axes of the slice: x: 4, y: 4 (y_hi: 2, y_lo: 2; y = y_hi * 2 + y_lo), z: 4, core: 2. Of those that a mesh axis runs over, the one named last changes fastest.
Arguments:
- tokens: bfloat16 [8192, 2048], P('dp'), may hold values from -6 to 6
- routes: int32 [8192, 8], P('dp'), may hold values from 0 to 127, all different within a row; in each aligned block of 128 rows (0 to 127, 128 to 255, ...) at most 12 rows name the same one
- probs: float32 [8192, 8], P('dp'), may hold values from 0.1 to 1
- w_gate: bfloat16 [128, 2048, 768], P('dp', None, 'col'), may hold values from -0.125 to 0.125
- w_up: bfloat16 [128, 2048, 768], P('dp', None, 'col'), may hold values from -0.125 to 0.125
- w_down: bfloat16 [128, 768, 2048], P('dp', 'col'), may hold values from -0.21875 to 0.21875
- cotangent: bfloat16 [8192, 2048], P('dp', 'col'), may hold values from -6 to 6
Outputs:
- mixed: bfloat16 [8192, 2048], P('dp', 'col')
- grad_tokens: bfloat16 [8192, 2048], P('dp', 'col')
- grad_probs: float32 [8192, 8], P('dp')
- grad_gate: bfloat16 [128, 2048, 768], P('dp', None, 'col')
- grad_up: bfloat16 [128, 2048, 768], P('dp', None, 'col')
- grad_down: bfloat16 [128, 768, 2048], P('dp', 'col')
The draws below stay inside these ranges and needn't reach their ends.
Inputs may be any that keep to these rules, and one draw needn't show every extreme that they name: `routes`: each token names 8 different experts. Among the 128 tokens of one index of dp, no expert is named by more than 12 of them, a bound that some block reaches.
All inputs are finite; a program needn't handle non-finite values.
Results may differ from the reference program's by a relative error of at most 0.0064.
Values may be sent and summed in bfloat16 or wider, within the bound.
A program may use at most 192 MiB of HBM per device.

```python
import math
import jax
import jax.numpy as jnp
import numpy as np
from jax import lax

D = 2048
HID = 768
TOP = 8
TOK_DEV = 128
EXPERTS = 128
CAP = 12
TOKENS = 8192
N_DP = 64


def shard_levels(own_key, dims, shards, low, largest):
    factor_of, own = 1.0, jax.random.fold_in(own_key, 6)
    for axis_at, blocks in shards:
        steps = jnp.exp(jax.random.uniform(jax.random.fold_in(own, axis_at), (blocks,), jnp.float32, low / len(shards), largest / len(shards)))
        factor_of = factor_of * jnp.repeat(steps, dims[axis_at] // blocks).reshape([-1 if axis == axis_at else 1 for axis in range(len(dims))])
    return factor_of


def routed_block(rng, own, number, rows, amount, top, reach, slope):
    ranking = jax.random.permutation(rng, amount)
    heavy_load, usual = portions_of(amount, rows * top, reach, slope, True), portions_of(amount, rows * top, reach, slope, False)
    places = jnp.arange(amount)

    def named(lengths, turn):
        used = int((lengths > 0).sum())
        fixed = max(1, used // 4)
        shifted = fixed + (places - fixed + turn * (used - fixed)) % max(1, amount - fixed)
        return jnp.zeros((amount,), jnp.int32).at[ranking[jnp.where(places < fixed, places, shifted)]].set(jnp.asarray(lengths, jnp.int32))

    lengths = jnp.where(number % 4 == 0, named(heavy_load, number // 4), named(usual, number - number // 4 - 1))
    mixed = jax.random.permutation(jax.random.fold_in(own, 3), amount)
    source_of, taker = mixed[0:amount // 2 * 2:2], mixed[1:amount // 2 * 2:2]
    slack = jnp.minimum(lengths[source_of] - 1, reach - lengths[taker]) // 2
    slack = jnp.where((source_of == ranking[0]) | (taker == ranking[0]) | (lengths[taker] == 0), 0, jnp.maximum(slack, 0))
    shifted = jax.random.randint(jax.random.fold_in(own, 4), (amount // 2,), 0, 1 << 20) % (slack + 1)
    lengths = lengths.at[source_of].add(-shifted).at[taker].add(shifted)
    items = jnp.searchsorted(jnp.cumsum(lengths), jnp.arange(rows * top), side="right").astype(jnp.int32)
    table = items.reshape(top, rows).T
    table = table[jax.random.permutation(jax.random.fold_in(own, 1), rows)]
    turn = jax.random.randint(jax.random.fold_in(own, 2), (rows, 1), 0, top)
    return jnp.take_along_axis(table, (jnp.arange(top)[None, :] + turn) % top, axis=1)


def portions_of(number_of, total, reach, slope, full):
    weights = [(1 << 20) // math.isqrt(rank ** slope) + 1 for rank in range(1, number_of + 1)]
    largest = reach if full else min(reach, max(-(-total // number_of), total * weights[0] // sum(weights)))
    least = 1 if total - largest >= number_of - 1 else 0
    counts, surplus = [largest] + [least] * (number_of - 1), total - largest - least * (number_of - 1)
    while surplus > 0:
        candidates = [i for i in range(1, number_of) if counts[i] < largest] or [i for i in range(1, number_of) if counts[i] < reach]
        whole, budget = sum([weights[i] for i in candidates]), surplus
        for i in candidates:
            extra = min(reach - counts[i], max(1, budget * weights[i] // whole), surplus)
            counts[i] = counts[i] + extra
            surplus = surplus - extra
    return np.array(counts)


def noise(stream_key, shape, deviation, most, cuts=(), held_as=jnp.bfloat16):
    entries = deviation * jax.random.normal(stream_key, shape, jnp.float32)
    if cuts:
        entries = entries * shard_levels(stream_key, shape, cuts, -0.22, 0.18)
    return jnp.clip(entries, -most, most).astype(held_as)


def setup_inputs(seed: int = 0) -> dict:
    key_of = jax.random.split(jax.random.key(seed), 8)
    tokens = noise(key_of[0], (TOKENS, D), 1.0, 6.0, ((0, 64),))
    routes_keys = jax.random.split(jax.random.fold_in(key_of[1], 1), TOKENS // TOK_DEV)
    routes_turns = jax.random.permutation(jax.random.fold_in(key_of[1], 3), TOKENS // TOK_DEV)
    routes = jax.vmap(lambda own, number: routed_block(jax.random.fold_in(key_of[1], 2), own, number, TOK_DEV, EXPERTS, TOP, CAP, 2))(routes_keys, routes_turns).reshape((TOKENS, TOP))
    probs = jnp.clip(0.1 + 0.9 * jax.random.uniform(key_of[2], (TOKENS, TOP), jnp.float32) ** shard_levels(key_of[2], (TOKENS, TOP), ((0, 64),), -0.2, 0.2), 0.1, 1.0)
    w_gate = noise(key_of[3], (EXPERTS, D, HID), D ** -0.5, 0.125, ((0, 64), (2, 2)))
    w_up = noise(key_of[4], (EXPERTS, D, HID), D ** -0.5, 0.125, ((0, 64), (2, 2)))
    w_down = noise(key_of[5], (EXPERTS, HID, D), HID ** -0.5, 0.21875, ((0, 64), (1, 2)))
    cotangent = noise(key_of[6], (TOKENS, D), 1.0, 6.0, ((0, 64), (1, 2)))
    return dict(tokens=tokens, routes=routes, probs=probs, w_gate=w_gate, w_up=w_up, w_down=w_down, cotangent=cotangent)


def slot_numbers(route_block):
    expert_ids = jnp.arange(EXPERTS, dtype=jnp.int32)
    onehot = (route_block[:, None] == expert_ids[None, :]).astype(jnp.int32)
    before = jnp.cumsum(onehot, axis=0) - onehot
    return jnp.sum(before * onehot, axis=1).astype(jnp.int32)


def reference(tokens, routes, probs, w_gate, w_up, w_down, cotangent):
    pair_count = TOK_DEV * TOP
    flat_routes = routes.reshape(N_DP, pair_count)
    slot_table = lax.map(slot_numbers, flat_routes)
    position = (flat_routes * CAP + slot_table).astype(jnp.int32)
    pair_ids = jnp.arange(N_DP * pair_count, dtype=jnp.int32).reshape(N_DP, pair_count)
    source_ids = jnp.arange(N_DP, dtype=jnp.int32)[:, None] + jnp.zeros((1, pair_count), jnp.int32)
    pair_table = jnp.full((N_DP, EXPERTS * CAP), -1, jnp.int32)
    pair_table = pair_table.at[source_ids, position].set(pair_ids)
    pair_table = pair_table.reshape(N_DP, EXPERTS, CAP).transpose(1, 0, 2).reshape(EXPERTS, N_DP * CAP)
    prob_flat = probs.reshape(-1)

    def one_expert(totals, inputs):
        mixed_acc, grad_acc, prob_acc = totals
        pair_list, gate_w, up_w, down_w = inputs
        is_valid = pair_list >= 0
        safe_pairs = jnp.where(is_valid, pair_list, 0).astype(jnp.int32)
        token_idx = (safe_pairs // TOP).astype(jnp.int32)
        pair_weight = jnp.where(is_valid, prob_flat[safe_pairs], 0.0 * prob_flat[0])
        row_block = jnp.where(is_valid[:, None], tokens[token_idx], jnp.zeros_like(tokens[:1]))
        gate_acts = jnp.dot(row_block, gate_w, preferred_element_type=jnp.float32)
        up_acts = jnp.dot(row_block, up_w, preferred_element_type=jnp.float32)
        sigmoid_g = jax.nn.sigmoid(gate_acts)
        silu_g = gate_acts * sigmoid_g
        hidden = (silu_g * up_acts).astype(jnp.bfloat16)
        out_rows = jnp.dot(hidden, down_w, preferred_element_type=jnp.float32).astype(jnp.bfloat16)
        cot_rows = cotangent[token_idx].astype(jnp.float32)
        d_out = (pair_weight[:, None] * cot_rows).astype(jnp.bfloat16)
        grad_down = jnp.dot(hidden.T, d_out, preferred_element_type=jnp.float32).astype(jnp.bfloat16)
        d_hidden = jnp.dot(d_out, down_w.T, preferred_element_type=jnp.float32)
        d_gate = (d_hidden * up_acts * sigmoid_g * (1.0 + gate_acts * (1.0 - sigmoid_g))).astype(jnp.bfloat16)
        d_up = (d_hidden * silu_g).astype(jnp.bfloat16)
        grad_gate = jnp.dot(row_block.T, d_gate, preferred_element_type=jnp.float32).astype(jnp.bfloat16)
        grad_up = jnp.dot(row_block.T, d_up, preferred_element_type=jnp.float32).astype(jnp.bfloat16)
        d_rows = (jnp.dot(d_gate, gate_w.T, preferred_element_type=jnp.float32)
                  + jnp.dot(d_up, up_w.T, preferred_element_type=jnp.float32)).astype(jnp.bfloat16)
        out_wide = out_rows.astype(jnp.float32)
        mixed_acc = mixed_acc.at[token_idx].add(pair_weight[:, None] * out_wide)
        grad_acc = grad_acc.at[token_idx].add(jnp.where(is_valid[:, None], d_rows.astype(jnp.float32), jnp.zeros_like(out_wide)))
        prob_terms = jnp.where(is_valid, jnp.sum(cot_rows * out_wide, axis=1), jnp.zeros_like(pair_weight))
        prob_acc = prob_acc.at[safe_pairs].add(prob_terms)
        return (mixed_acc, grad_acc, prob_acc), (grad_gate, grad_up, grad_down)

    start_totals = (jnp.zeros((TOKENS, D), jnp.float32), jnp.zeros((TOKENS, D), jnp.float32),
                    jnp.zeros((TOKENS * TOP,), jnp.float32))
    totals, grads = lax.scan(one_expert, start_totals, (pair_table, w_gate, w_up, w_down))
    mixed_acc, grad_acc, prob_acc = totals
    grad_gate, grad_up, grad_down = grads
    return (mixed_acc.astype(jnp.bfloat16), grad_acc.astype(jnp.bfloat16), prob_acc.reshape(TOKENS, TOP),
            grad_gate, grad_up, grad_down)
```

```python
import jax
import jax.numpy as jnp
from jax import lax
from jax.sharding import PartitionSpec as P


def body(tokens, routes, probs, w_gate, w_up, w_down, cotangent):
    tok_count, width = tokens.shape
    top_count = routes.shape[1]
    owners = lax.axis_size("dp")
    cols = lax.axis_size("col")
    local_experts = w_gate.shape[0]
    experts = local_experts * owners
    slot_cap = 3 * tok_count * top_count // (2 * experts)
    half_width = width // cols
    pair_count = tok_count * top_count
    rows_per_owner = local_experts * slot_cap
    slots = experts * slot_cap

    flat_routes = routes.reshape(-1)
    expert_ids = jnp.arange(experts, dtype=jnp.int32)
    onehot = (flat_routes[:, None] == expert_ids[None, :]).astype(jnp.int32)
    before = jnp.cumsum(onehot, axis=0) - onehot
    slot_index = jnp.sum(before * onehot, axis=1)
    flat_index = flat_routes * slot_cap + slot_index

    pair_of_slot = jnp.full((slots,), pair_count, jnp.int32).at[flat_index].set(
        jnp.arange(pair_count, dtype=jnp.int32)
    )
    valid = pair_of_slot < pair_count
    safe_pair = jnp.where(valid, pair_of_slot, 0)
    token_of_slot = safe_pair // top_count

    both = ("dp", "col")

    send_tok = jnp.where(valid[:, None], tokens[token_of_slot], jnp.zeros((), tokens.dtype))
    arrived_rows = lax.all_to_all(
        send_tok.reshape(owners, rows_per_owner, width), "dp", 0, 0, tiled=True
    )
    row_block = arrived_rows.reshape(owners, local_experts, slot_cap, width)

    prob_of_slot = jnp.where(valid, probs.reshape(-1)[safe_pair], 0.0)
    send_cot = (prob_of_slot[:, None] * cotangent[token_of_slot].astype(jnp.float32)).astype(
        jnp.bfloat16
    )
    send_cot = jnp.broadcast_to(
        send_cot.reshape(owners, 1, rows_per_owner, half_width),
        (owners, cols, rows_per_owner, half_width),
    ).reshape(owners * cols, rows_per_owner, half_width)
    arrived_cot = lax.all_to_all(send_cot, both, 0, 0, tiled=True)
    d_out = (
        arrived_cot.reshape(owners, cols, rows_per_owner, half_width)
        .transpose(0, 2, 1, 3)
        .reshape(owners, local_experts, slot_cap, width)
    )

    def send_back(partial_value):
        part = partial_value.astype(jnp.bfloat16).reshape(owners, rows_per_owner, cols, half_width)
        part = part.transpose(0, 2, 1, 3).reshape(owners * cols, rows_per_owner, half_width)
        got = lax.all_to_all(part, both, 0, 0, tiled=True)
        got = got.reshape(owners, cols, rows_per_owner, half_width).astype(jnp.float32)
        summed = jnp.sum(got, axis=1).reshape(slots, half_width)
        return summed[flat_index].reshape(tok_count, top_count, half_width)

    gate_acts = jnp.einsum("slcd,ldh->slch", row_block, w_gate, preferred_element_type=jnp.float32)
    up_acts = jnp.einsum("slcd,ldh->slch", row_block, w_up, preferred_element_type=jnp.float32)
    sigmoid_g = jax.nn.sigmoid(gate_acts)
    silu_g = gate_acts * sigmoid_g
    hidden = (silu_g * up_acts).astype(jnp.bfloat16)
    out_partial = jnp.einsum("slch,lhd->slcd", hidden, w_down, preferred_element_type=jnp.float32)
    picked_wide = send_back(out_partial)
    mixed = jnp.sum(probs[:, :, None] * picked_wide, axis=1).astype(jnp.bfloat16)
    cot_wide = cotangent.astype(jnp.float32)
    prob_part = jnp.sum(cot_wide[:, None, :] * picked_wide, axis=2)

    grad_down = jnp.einsum(
        "slch,slcd->lhd", hidden, d_out, preferred_element_type=jnp.float32
    ).astype(jnp.bfloat16)
    d_hidden = jnp.einsum("slcd,lhd->slch", d_out, w_down, preferred_element_type=jnp.float32)
    d_gate = (d_hidden * up_acts * sigmoid_g * (1.0 + gate_acts * (1.0 - sigmoid_g))).astype(
        jnp.bfloat16
    )
    d_up = (d_hidden * silu_g).astype(jnp.bfloat16)
    grad_gate = jnp.einsum(
        "slcd,slch->ldh", row_block, d_gate, preferred_element_type=jnp.float32
    ).astype(jnp.bfloat16)
    grad_up = jnp.einsum(
        "slcd,slch->ldh", row_block, d_up, preferred_element_type=jnp.float32
    ).astype(jnp.bfloat16)
    d_partial = jnp.einsum(
        "slch,ldh->slcd", d_gate, w_gate, preferred_element_type=jnp.float32
    ) + jnp.einsum("slch,ldh->slcd", d_up, w_up, preferred_element_type=jnp.float32)
    picked_grad = send_back(d_partial)
    grad_tokens = jnp.sum(picked_grad, axis=1).astype(jnp.bfloat16)
    grad_probs = lax.psum(prob_part, "col")
    return (mixed, grad_tokens, grad_probs, grad_gate, grad_up, grad_down)


def solution(mesh):
    return jax.shard_map(
        body,
        mesh=mesh,
        in_specs=(
            P("dp", None),
            P("dp", None),
            P("dp", None),
            P("dp", None, "col"),
            P("dp", None, "col"),
            P("dp", "col", None),
            P("dp", "col"),
        ),
        out_specs=(
            P("dp", "col"),
            P("dp", "col"),
            P("dp", None),
            P("dp", None, "col"),
            P("dp", None, "col"),
            P("dp", "col", None),
        ),
        check_vma=False,
    )
```

```python
import jax
import jax.numpy as jnp
from jax import lax
from jax.sharding import PartitionSpec as P


def body(tokens, routes, probs, w_gate, w_up, w_down, cotangent):
    tok_count, width = tokens.shape
    top_count = routes.shape[1]
    owners = lax.axis_size("dp")
    cols = lax.axis_size("col")
    local_experts = w_gate.shape[0]
    experts = local_experts * owners
    slot_cap = 3 * tok_count * top_count // (2 * experts)
    half_width = width // cols
    pair_count = tok_count * top_count
    rows_per_owner = local_experts * slot_cap
    slots = experts * slot_cap

    flat_routes = routes.reshape(-1)
    expert_ids = jnp.arange(experts, dtype=jnp.int32)
    onehot = (flat_routes[:, None] == expert_ids[None, :]).astype(jnp.int32)
    before = jnp.cumsum(onehot, axis=0) - onehot
    slot_index = jnp.sum(before * onehot, axis=1)
    flat_index = flat_routes * slot_cap + slot_index

    slot_ids = jnp.arange(slots, dtype=jnp.int32)
    match = flat_index.reshape(tok_count, top_count)[:, :, None] == slot_ids[None, None, :]
    weight = jnp.sum(jnp.where(match, probs[:, :, None], 0.0), axis=1)
    taken = jnp.any(match, axis=1)
    picker = taken.astype(jnp.bfloat16)
    weight_hi = weight.astype(jnp.bfloat16)
    weight_lo = (weight - weight_hi.astype(jnp.float32)).astype(jnp.bfloat16)
    prob_of_slot = jnp.sum(weight, axis=0)

    both = ("dp", "col")

    send_tok = jnp.einsum(
        "ts,td->sd", picker, tokens, preferred_element_type=jnp.float32
    ).astype(jnp.bfloat16)
    arrived_rows = lax.all_to_all(
        send_tok.reshape(owners, rows_per_owner, width), "dp", 0, 0, tiled=True
    )
    row_block = arrived_rows.reshape(owners, local_experts, slot_cap, width)

    cot_rows = jnp.einsum("ts,td->sd", picker, cotangent, preferred_element_type=jnp.float32)
    send_cot = (prob_of_slot[:, None] * cot_rows).astype(jnp.bfloat16)
    send_cot = jnp.broadcast_to(
        send_cot.reshape(owners, 1, rows_per_owner, half_width),
        (owners, cols, rows_per_owner, half_width),
    ).reshape(owners * cols, rows_per_owner, half_width)
    arrived_cot = lax.all_to_all(send_cot, both, 0, 0, tiled=True)
    d_out = (
        arrived_cot.reshape(owners, cols, rows_per_owner, half_width)
        .transpose(0, 2, 1, 3)
        .reshape(owners, local_experts, slot_cap, width)
    )

    def per_half(table):
        return jnp.broadcast_to(
            table.reshape(tok_count, owners, 1, rows_per_owner),
            (tok_count, owners, cols, rows_per_owner),
        )

    def send_back(partial_value):
        part = partial_value.astype(jnp.bfloat16).reshape(owners, rows_per_owner, cols, half_width)
        part = part.transpose(0, 2, 1, 3).reshape(owners * cols, rows_per_owner, half_width)
        got = lax.all_to_all(part, both, 0, 0, tiled=True)
        return got.reshape(owners, cols, rows_per_owner, half_width)

    def combine(table, got):
        return jnp.einsum("tocr,ocrd->td", per_half(table), got, preferred_element_type=jnp.float32)

    gate_acts = jnp.einsum("slcd,ldh->slch", row_block, w_gate, preferred_element_type=jnp.float32)
    up_acts = jnp.einsum("slcd,ldh->slch", row_block, w_up, preferred_element_type=jnp.float32)
    sigmoid_g = jax.nn.sigmoid(gate_acts)
    silu_g = gate_acts * sigmoid_g
    hidden = (silu_g * up_acts).astype(jnp.bfloat16)
    out_partial = jnp.einsum("slch,lhd->slcd", hidden, w_down, preferred_element_type=jnp.float32)
    got_out = send_back(out_partial)
    mixed = (combine(weight_hi, got_out) + combine(weight_lo, got_out)).astype(jnp.bfloat16)
    dots = jnp.einsum("td,ocrd->tocr", cotangent, got_out, preferred_element_type=jnp.float32)
    dots = jnp.sum(dots, axis=2).reshape(tok_count, 1, slots)
    prob_part = jnp.sum(jnp.where(match, dots, 0.0), axis=2)

    grad_down = jnp.einsum(
        "slch,slcd->lhd", hidden, d_out, preferred_element_type=jnp.float32
    ).astype(jnp.bfloat16)
    d_hidden = jnp.einsum("slcd,lhd->slch", d_out, w_down, preferred_element_type=jnp.float32)
    d_gate = (d_hidden * up_acts * sigmoid_g * (1.0 + gate_acts * (1.0 - sigmoid_g))).astype(
        jnp.bfloat16
    )
    d_up = (d_hidden * silu_g).astype(jnp.bfloat16)
    grad_gate = jnp.einsum(
        "slcd,slch->ldh", row_block, d_gate, preferred_element_type=jnp.float32
    ).astype(jnp.bfloat16)
    grad_up = jnp.einsum(
        "slcd,slch->ldh", row_block, d_up, preferred_element_type=jnp.float32
    ).astype(jnp.bfloat16)
    d_partial = jnp.einsum(
        "slch,ldh->slcd", d_gate, w_gate, preferred_element_type=jnp.float32
    ) + jnp.einsum("slch,ldh->slcd", d_up, w_up, preferred_element_type=jnp.float32)
    got_grad = send_back(d_partial)
    grad_tokens = combine(picker, got_grad).astype(jnp.bfloat16)
    grad_probs = prob_part + lax.ppermute(prob_part, "col", perm=[(0, 1), (1, 0)])
    return (mixed, grad_tokens, grad_probs, grad_gate, grad_up, grad_down)


def solution(mesh):
    return jax.shard_map(
        body,
        mesh=mesh,
        in_specs=(
            P("dp", None),
            P("dp", None),
            P("dp", None),
            P("dp", None, "col"),
            P("dp", None, "col"),
            P("dp", "col", None),
            P("dp", "col"),
        ),
        out_specs=(
            P("dp", "col"),
            P("dp", "col"),
            P("dp", None),
            P("dp", None, "col"),
            P("dp", None, "col"),
            P("dp", "col", None),
        ),
        check_vma=False,
    )
```

```python
import jax
import jax.numpy as jnp
from jax import lax
from jax.sharding import PartitionSpec as P


def body(tokens, routes, probs, w_gate, w_up, w_down, cotangent):
    tok_count, width = tokens.shape
    top_count = routes.shape[1]
    owners = lax.axis_size("dp")
    cols = lax.axis_size("col")
    local_experts = w_gate.shape[0]
    experts = local_experts * owners
    slot_cap = 3 * tok_count * top_count // (2 * experts)
    half_width = width // cols
    pair_count = tok_count * top_count
    rows_per_owner = local_experts * slot_cap
    slots = experts * slot_cap

    flat_routes = routes.reshape(-1)
    expert_ids = jnp.arange(experts, dtype=jnp.int32)
    onehot = (flat_routes[:, None] == expert_ids[None, :]).astype(jnp.int32)
    before = jnp.cumsum(onehot, axis=0) - onehot
    slot_index = jnp.sum(before * onehot, axis=1)
    flat_index = flat_routes * slot_cap + slot_index

    slot_ids = jnp.arange(slots, dtype=jnp.int32)
    match = flat_index.reshape(tok_count, top_count)[:, :, None] == slot_ids[None, None, :]
    weight = jnp.sum(jnp.where(match, probs[:, :, None], 0.0), axis=1)
    taken = jnp.any(match, axis=1)
    picker = taken.astype(jnp.bfloat16)
    weight_hi = weight.astype(jnp.bfloat16)
    weight_lo = (weight - weight_hi.astype(jnp.float32)).astype(jnp.bfloat16)
    prob_of_slot = jnp.sum(weight, axis=0)

    both = ("dp", "col")

    send_tok = jnp.einsum(
        "ts,td->sd", picker, tokens, preferred_element_type=jnp.float32
    ).astype(jnp.bfloat16)
    arrived_rows = lax.all_to_all(
        send_tok.reshape(owners, rows_per_owner, width), "dp", 0, 0, tiled=True
    )
    row_block = arrived_rows.reshape(owners, local_experts, slot_cap, width)

    cot_rows = jnp.einsum("ts,td->sd", picker, cotangent, preferred_element_type=jnp.float32)
    send_cot = (prob_of_slot[:, None] * cot_rows).astype(jnp.bfloat16)
    send_cot = jnp.broadcast_to(
        send_cot.reshape(owners, 1, rows_per_owner, half_width),
        (owners, cols, rows_per_owner, half_width),
    ).reshape(owners * cols, rows_per_owner, half_width)
    arrived_cot = lax.all_to_all(send_cot, both, 0, 0, tiled=True)
    arrived_rows, arrived_cot = lax.optimization_barrier((arrived_rows, arrived_cot))
    row_block = arrived_rows.reshape(owners, local_experts, slot_cap, width)
    d_out = (
        arrived_cot.reshape(owners, cols, rows_per_owner, half_width)
        .transpose(0, 2, 1, 3)
        .reshape(owners, local_experts, slot_cap, width)
    )

    def per_half(table):
        return jnp.broadcast_to(
            table.reshape(tok_count, owners, 1, rows_per_owner),
            (tok_count, owners, cols, rows_per_owner),
        )

    def send_back(partial_value):
        part = partial_value.astype(jnp.bfloat16).reshape(owners, rows_per_owner, cols, half_width)
        part = part.transpose(0, 2, 1, 3).reshape(owners * cols, rows_per_owner, half_width)
        got = lax.all_to_all(part, both, 0, 0, tiled=True)
        return got.reshape(owners, cols, rows_per_owner, half_width)

    def combine(table, got):
        return jnp.einsum("tocr,ocrd->td", per_half(table), got, preferred_element_type=jnp.float32)

    gate_acts = jnp.einsum("slcd,ldh->slch", row_block, w_gate, preferred_element_type=jnp.float32)
    up_acts = jnp.einsum("slcd,ldh->slch", row_block, w_up, preferred_element_type=jnp.float32)
    sigmoid_g = jax.nn.sigmoid(gate_acts)
    silu_g = gate_acts * sigmoid_g
    hidden = (silu_g * up_acts).astype(jnp.bfloat16)
    out_partial = jnp.einsum("slch,lhd->slcd", hidden, w_down, preferred_element_type=jnp.float32)
    got_out = send_back(out_partial)
    mixed = (combine(weight_hi, got_out) + combine(weight_lo, got_out)).astype(jnp.bfloat16)
    dots = jnp.einsum("td,ocrd->tocr", cotangent, got_out, preferred_element_type=jnp.float32)
    dots = jnp.sum(dots, axis=2).reshape(tok_count, 1, slots)
    prob_part = jnp.sum(jnp.where(match, dots, 0.0), axis=2)

    grad_down = jnp.einsum(
        "slch,slcd->lhd", hidden, d_out, preferred_element_type=jnp.float32
    ).astype(jnp.bfloat16)
    d_hidden = jnp.einsum("slcd,lhd->slch", d_out, w_down, preferred_element_type=jnp.float32)
    d_gate = (d_hidden * up_acts * sigmoid_g * (1.0 + gate_acts * (1.0 - sigmoid_g))).astype(
        jnp.bfloat16
    )
    d_up = (d_hidden * silu_g).astype(jnp.bfloat16)
    grad_gate = jnp.einsum(
        "slcd,slch->ldh", row_block, d_gate, preferred_element_type=jnp.float32
    ).astype(jnp.bfloat16)
    grad_up = jnp.einsum(
        "slcd,slch->ldh", row_block, d_up, preferred_element_type=jnp.float32
    ).astype(jnp.bfloat16)
    d_partial = jnp.einsum(
        "slch,ldh->slcd", d_gate, w_gate, preferred_element_type=jnp.float32
    ) + jnp.einsum("slch,ldh->slcd", d_up, w_up, preferred_element_type=jnp.float32)
    prob_other = lax.ppermute(prob_part, "col", perm=[(0, 1), (1, 0)])
    prob_other, d_partial = lax.optimization_barrier((prob_other, d_partial))
    got_grad = send_back(d_partial)
    grad_tokens = combine(picker, got_grad).astype(jnp.bfloat16)
    grad_probs = prob_part + prob_other
    return (mixed, grad_tokens, grad_probs, grad_gate, grad_up, grad_down)


def solution(mesh):
    return jax.shard_map(
        body,
        mesh=mesh,
        in_specs=(
            P("dp", None),
            P("dp", None),
            P("dp", None),
            P("dp", None, "col"),
            P("dp", None, "col"),
            P("dp", "col", None),
            P("dp", "col"),
        ),
        out_specs=(
            P("dp", "col"),
            P("dp", "col"),
            P("dp", None),
            P("dp", None, "col"),
            P("dp", None, "col"),
            P("dp", "col", None),
        ),
        check_vma=False,
    )
```

```python
import jax
import jax.numpy as jnp
from jax import lax
from jax.experimental import pallas as pl
from jax.experimental.pallas import tpu as pltpu
from jax.sharding import PartitionSpec as P

MESH_ID = pl.DeviceIdType.MESH


def _where(me_dp, me_col):
    return me_dp * 2 + me_col


def _dispatch_kernel(tok_ref, cot_ref, rows_ref, dout_ref, send_sems, recv_sems):
    owners, rows, half = tok_ref.shape
    me_dp, me_col = lax.axis_index("dp"), lax.axis_index("col")
    count = owners * 2
    me = _where(me_dp, me_col)
    here = pl.ds(pl.multiple_of(me_col * half, half), half)
    srcs, dsts = (tok_ref, cot_ref), (rows_ref, dout_ref)

    def remote(kind, target):
        t_dp, t_col = target // 2, target % 2
        return pltpu.make_async_remote_copy(
            src_ref=srcs[kind].at[t_dp],
            dst_ref=dsts[kind].at[me_dp, :, here],
            send_sem=send_sems.at[kind, target],
            recv_sem=recv_sems.at[kind, me],
            device_id=(t_dp, t_col),
            device_id_type=MESH_ID,
        )

    def incoming(kind, source):
        s_dp, s_col = source // 2, source % 2
        there = pl.ds(pl.multiple_of(s_col * half, half), half)
        return pltpu.make_async_remote_copy(
            src_ref=srcs[kind].at[0],
            dst_ref=dsts[kind].at[s_dp, :, there],
            send_sem=send_sems.at[kind, source],
            recv_sem=recv_sems.at[kind, source],
            device_id=(s_dp, s_col),
            device_id_type=MESH_ID,
        )

    for kind in range(2):
        pltpu.make_async_copy(
            srcs[kind].at[me_dp], dsts[kind].at[me_dp, :, here], recv_sems.at[kind, me]
        ).start()

    def start(i, carry):
        target = lax.rem(me + i, count)
        for kind in range(2):
            remote(kind, target).start()
        return carry

    lax.fori_loop(1, count, start, 0)

    def finish(i, carry):
        other = lax.rem(me + i, count)
        for kind in range(2):
            remote(kind, other).wait_send()
            incoming(kind, other).wait_recv()
        return carry

    lax.fori_loop(1, count, finish, 0)
    for kind in range(2):
        pltpu.make_async_copy(
            srcs[kind].at[me_dp], dsts[kind].at[me_dp, :, here], recv_sems.at[kind, me]
        ).wait()


def _return_kernel(part_ref, recv_ref, send_sems, recv_sems):
    sources, rows, width = part_ref.shape
    half = width // 2
    me_dp, me_col = lax.axis_index("dp"), lax.axis_index("col")
    count = sources * 2
    me = _where(me_dp, me_col)

    def window(target):
        cols = pl.ds(pl.multiple_of((target % 2) * half, half), half)
        return part_ref.at[target // 2, :, cols]

    def remote(target):
        return pltpu.make_async_remote_copy(
            src_ref=window(target),
            dst_ref=recv_ref.at[me],
            send_sem=send_sems.at[target],
            recv_sem=recv_sems.at[me],
            device_id=(target // 2, target % 2),
            device_id_type=MESH_ID,
        )

    def incoming(source):
        return pltpu.make_async_remote_copy(
            src_ref=window(source),
            dst_ref=recv_ref.at[source],
            send_sem=send_sems.at[source],
            recv_sem=recv_sems.at[source],
            device_id=(source // 2, source % 2),
            device_id_type=MESH_ID,
        )

    pltpu.make_async_copy(window(me), recv_ref.at[me], recv_sems.at[me]).start()

    def start(i, carry):
        remote(lax.rem(me + i, count)).start()
        return carry

    lax.fori_loop(1, count, start, 0)

    def finish(i, carry):
        other = lax.rem(me + i, count)
        remote(other).wait_send()
        incoming(other).wait_recv()
        return carry

    lax.fori_loop(1, count, finish, 0)
    pltpu.make_async_copy(window(me), recv_ref.at[me], recv_sems.at[me]).wait()


def dispatch(tok_half, cot_half):
    owners, rows, half = tok_half.shape
    full = jax.ShapeDtypeStruct((owners, rows, 2 * half), tok_half.dtype)
    return pl.pallas_call(
        _dispatch_kernel,
        out_shape=(full, full),
        in_specs=[pl.BlockSpec(memory_space=pl.ANY)] * 2,
        out_specs=(pl.BlockSpec(memory_space=pl.ANY),) * 2,
        scratch_shapes=[
            pltpu.SemaphoreType.DMA((2, owners * 2)),
            pltpu.SemaphoreType.DMA((2, owners * 2)),
        ],
        compiler_params=pltpu.CompilerParams(has_side_effects=True),
    )(tok_half, cot_half)


def send_home(part):
    sources, rows, width = part.shape
    return pl.pallas_call(
        _return_kernel,
        out_shape=jax.ShapeDtypeStruct((sources * 2, rows, width // 2), part.dtype),
        in_specs=[pl.BlockSpec(memory_space=pl.ANY)],
        out_specs=pl.BlockSpec(memory_space=pl.ANY),
        scratch_shapes=[
            pltpu.SemaphoreType.DMA((sources * 2,)),
            pltpu.SemaphoreType.DMA((sources * 2,)),
        ],
        compiler_params=pltpu.CompilerParams(has_side_effects=True),
    )(part)


def body(tokens, routes, probs, w_gate, w_up, w_down, cotangent):
    tok_count, width = tokens.shape
    top_count = routes.shape[1]
    owners = lax.axis_size("dp")
    cols = lax.axis_size("col")
    local_experts = w_gate.shape[0]
    experts = local_experts * owners
    slot_cap = 3 * tok_count * top_count // (2 * experts)
    half_width = width // cols
    pair_count = tok_count * top_count
    rows_per_owner = local_experts * slot_cap
    slots = experts * slot_cap

    flat_routes = routes.reshape(-1)
    expert_ids = jnp.arange(experts, dtype=jnp.int32)
    onehot = (flat_routes[:, None] == expert_ids[None, :]).astype(jnp.int32)
    before = jnp.cumsum(onehot, axis=0) - onehot
    slot_index = jnp.sum(before * onehot, axis=1)
    flat_index = flat_routes * slot_cap + slot_index

    slot_ids = jnp.arange(slots, dtype=jnp.int32)
    match = flat_index.reshape(tok_count, top_count)[:, :, None] == slot_ids[None, None, :]
    weight = jnp.sum(jnp.where(match, probs[:, :, None], 0.0), axis=1)
    taken = jnp.any(match, axis=1)
    picker = taken.astype(jnp.bfloat16)
    weight_hi = weight.astype(jnp.bfloat16)
    weight_lo = (weight - weight_hi.astype(jnp.float32)).astype(jnp.bfloat16)
    prob_of_slot = jnp.sum(weight, axis=0)

    both = ("dp", "col")

    my_cols = lax.axis_index("col") * half_width
    tok_half = lax.dynamic_slice_in_dim(tokens, my_cols, half_width, axis=1)
    send_tok = jnp.einsum(
        "ts,td->sd", picker, tok_half, preferred_element_type=jnp.float32
    ).astype(jnp.bfloat16)
    cot_rows = jnp.einsum("ts,td->sd", picker, cotangent, preferred_element_type=jnp.float32)
    send_cot = (prob_of_slot[:, None] * cot_rows).astype(jnp.bfloat16)
    arrived_rows, arrived_cot = dispatch(
        send_tok.reshape(owners, rows_per_owner, half_width),
        send_cot.reshape(owners, rows_per_owner, half_width),
    )
    row_block = arrived_rows.reshape(owners, local_experts, slot_cap, width)
    d_out = arrived_cot.reshape(owners, local_experts, slot_cap, width)

    def per_half(table):
        return jnp.broadcast_to(
            table.reshape(tok_count, owners, 1, rows_per_owner),
            (tok_count, owners, cols, rows_per_owner),
        )

    def send_back(partial_value):
        part = partial_value.astype(jnp.bfloat16).reshape(owners, rows_per_owner, width)
        return send_home(part).reshape(owners, cols, rows_per_owner, half_width)

    def combine(table, got):
        return jnp.einsum("tocr,ocrd->td", per_half(table), got, preferred_element_type=jnp.float32)

    gate_acts = jnp.einsum("slcd,ldh->slch", row_block, w_gate, preferred_element_type=jnp.float32)
    up_acts = jnp.einsum("slcd,ldh->slch", row_block, w_up, preferred_element_type=jnp.float32)
    sigmoid_g = jax.nn.sigmoid(gate_acts)
    silu_g = gate_acts * sigmoid_g
    hidden = (silu_g * up_acts).astype(jnp.bfloat16)
    out_partial = jnp.einsum("slch,lhd->slcd", hidden, w_down, preferred_element_type=jnp.float32)
    got_out = send_back(out_partial)
    mixed = (combine(weight_hi, got_out) + combine(weight_lo, got_out)).astype(jnp.bfloat16)
    dots = jnp.einsum("td,ocrd->tocr", cotangent, got_out, preferred_element_type=jnp.float32)
    dots = jnp.sum(dots, axis=2).reshape(tok_count, 1, slots)
    prob_part = jnp.sum(jnp.where(match, dots, 0.0), axis=2)

    grad_down = jnp.einsum(
        "slch,slcd->lhd", hidden, d_out, preferred_element_type=jnp.float32
    ).astype(jnp.bfloat16)
    d_hidden = jnp.einsum("slcd,lhd->slch", d_out, w_down, preferred_element_type=jnp.float32)
    d_gate = (d_hidden * up_acts * sigmoid_g * (1.0 + gate_acts * (1.0 - sigmoid_g))).astype(
        jnp.bfloat16
    )
    d_up = (d_hidden * silu_g).astype(jnp.bfloat16)
    grad_gate = jnp.einsum(
        "slcd,slch->ldh", row_block, d_gate, preferred_element_type=jnp.float32
    ).astype(jnp.bfloat16)
    grad_up = jnp.einsum(
        "slcd,slch->ldh", row_block, d_up, preferred_element_type=jnp.float32
    ).astype(jnp.bfloat16)
    d_partial = jnp.einsum(
        "slch,ldh->slcd", d_gate, w_gate, preferred_element_type=jnp.float32
    ) + jnp.einsum("slch,ldh->slcd", d_up, w_up, preferred_element_type=jnp.float32)
    prob_other = lax.ppermute(prob_part, "col", perm=[(0, 1), (1, 0)])
    got_grad = send_back(d_partial)
    grad_tokens = combine(picker, got_grad).astype(jnp.bfloat16)
    grad_probs = prob_part + prob_other
    return (mixed, grad_tokens, grad_probs, grad_gate, grad_up, grad_down)


def solution(mesh):
    return jax.shard_map(
        body,
        mesh=mesh,
        in_specs=(
            P("dp", None),
            P("dp", None),
            P("dp", None),
            P("dp", None, "col"),
            P("dp", None, "col"),
            P("dp", "col", None),
            P("dp", "col"),
        ),
        out_specs=(
            P("dp", "col"),
            P("dp", "col"),
            P("dp", None),
            P("dp", None, "col"),
            P("dp", None, "col"),
            P("dp", "col", None),
        ),
        check_vma=False,
    )
```

```python
import jax
import jax.numpy as jnp
from jax import lax
from jax.sharding import PartitionSpec as P


def body(tokens, routes, probs, w_gate, w_up, w_down, cotangent):
    tok_count, width = tokens.shape
    top_count = routes.shape[1]
    owners = lax.axis_size("dp")
    cols = lax.axis_size("col")
    local_experts = w_gate.shape[0]
    experts = local_experts * owners
    slot_cap = 3 * tok_count * top_count // (2 * experts)
    half_width = width // cols
    pair_count = tok_count * top_count
    rows_per_owner = local_experts * slot_cap
    slots = experts * slot_cap

    flat_routes = routes.reshape(-1)
    expert_ids = jnp.arange(experts, dtype=jnp.int32)
    onehot = (flat_routes[:, None] == expert_ids[None, :]).astype(jnp.int32)
    before = jnp.cumsum(onehot, axis=0) - onehot
    slot_index = jnp.sum(before * onehot, axis=1)
    flat_index = flat_routes * slot_cap + slot_index

    pair_of_slot = jnp.full((slots,), pair_count, jnp.int32).at[flat_index].set(
        jnp.arange(pair_count, dtype=jnp.int32)
    )
    valid = pair_of_slot < pair_count
    safe_pair = jnp.where(valid, pair_of_slot, 0)
    token_of_slot = safe_pair // top_count

    both = ("dp", "col")

    send_tok = jnp.where(valid[:, None], tokens[token_of_slot], jnp.zeros((), tokens.dtype))
    arrived_rows = lax.all_to_all(
        send_tok.reshape(owners, rows_per_owner, width), "dp", 0, 0, tiled=True
    )
    row_block = arrived_rows.reshape(owners, local_experts, slot_cap, width)

    prob_of_slot = jnp.where(valid, probs.reshape(-1)[safe_pair], 0.0)
    send_cot = (prob_of_slot[:, None] * cotangent[token_of_slot].astype(jnp.float32)).astype(
        jnp.bfloat16
    )
    send_cot = jnp.broadcast_to(
        send_cot.reshape(owners, 1, rows_per_owner, half_width),
        (owners, cols, rows_per_owner, half_width),
    ).reshape(owners * cols, rows_per_owner, half_width)
    arrived_cot = lax.all_to_all(send_cot, both, 0, 0, tiled=True)
    d_out = (
        arrived_cot.reshape(owners, cols, rows_per_owner, half_width)
        .transpose(0, 2, 1, 3)
        .reshape(owners, local_experts, slot_cap, width)
    )

    def send_back(partial_value):
        part = partial_value.astype(jnp.bfloat16).reshape(owners, rows_per_owner, cols, half_width)
        part = part.transpose(0, 2, 1, 3).reshape(owners * cols, rows_per_owner, half_width)
        got = lax.all_to_all(part, both, 0, 0, tiled=True)
        got = got.reshape(owners, cols, rows_per_owner, half_width).astype(jnp.float32)
        summed = jnp.sum(got, axis=1).reshape(slots, half_width)
        return summed[flat_index].reshape(tok_count, top_count, half_width)

    gate_acts = jnp.einsum("slcd,ldh->slch", row_block, w_gate, preferred_element_type=jnp.float32)
    up_acts = jnp.einsum("slcd,ldh->slch", row_block, w_up, preferred_element_type=jnp.float32)
    sigmoid_g = jax.nn.sigmoid(gate_acts)
    silu_g = gate_acts * sigmoid_g
    hidden = (silu_g * up_acts).astype(jnp.bfloat16)
    out_partial = jnp.einsum("slch,lhd->slcd", hidden, w_down, preferred_element_type=jnp.float32)
    picked_wide = send_back(out_partial)
    mixed = jnp.sum(probs[:, :, None] * picked_wide, axis=1).astype(jnp.bfloat16)
    cot_wide = cotangent.astype(jnp.float32)
    prob_part = jnp.sum(cot_wide[:, None, :] * picked_wide, axis=2)

    grad_down = jnp.einsum(
        "slch,slcd->lhd", hidden, d_out, preferred_element_type=jnp.float32
    ).astype(jnp.bfloat16)
    d_hidden = jnp.einsum("slcd,lhd->slch", d_out, w_down, preferred_element_type=jnp.float32)
    d_gate = (d_hidden * up_acts * sigmoid_g * (1.0 + gate_acts * (1.0 - sigmoid_g))).astype(
        jnp.bfloat16
    )
    d_up = (d_hidden * silu_g).astype(jnp.bfloat16)
    grad_gate = jnp.einsum(
        "slcd,slch->ldh", row_block, d_gate, preferred_element_type=jnp.float32
    ).astype(jnp.bfloat16)
    grad_up = jnp.einsum(
        "slcd,slch->ldh", row_block, d_up, preferred_element_type=jnp.float32
    ).astype(jnp.bfloat16)
    d_partial = jnp.einsum(
        "slch,ldh->slcd", d_gate, w_gate, preferred_element_type=jnp.float32
    ) + jnp.einsum("slch,ldh->slcd", d_up, w_up, preferred_element_type=jnp.float32)
    prob_other = lax.ppermute(prob_part, "col", perm=[(0, 1), (1, 0)])
    prob_other, d_partial = lax.optimization_barrier((prob_other, d_partial))
    picked_grad = send_back(d_partial)
    grad_tokens = jnp.sum(picked_grad, axis=1).astype(jnp.bfloat16)
    grad_probs = prob_part + prob_other
    return (mixed, grad_tokens, grad_probs, grad_gate, grad_up, grad_down)


def solution(mesh):
    return jax.shard_map(
        body,
        mesh=mesh,
        in_specs=(
            P("dp", None),
            P("dp", None),
            P("dp", None),
            P("dp", None, "col"),
            P("dp", None, "col"),
            P("dp", "col", None),
            P("dp", "col"),
        ),
        out_specs=(
            P("dp", "col"),
            P("dp", "col"),
            P("dp", None),
            P("dp", None, "col"),
            P("dp", None, "col"),
            P("dp", "col", None),
        ),
        check_vma=False,
    )
```

```python
import jax
import jax.numpy as jnp
from jax import lax
from jax.sharding import PartitionSpec as P


def body(tokens, routes, probs, w_gate, w_up, w_down, cotangent):
    tok_count, width = tokens.shape
    top_count = routes.shape[1]
    owners = lax.axis_size("dp")
    cols = lax.axis_size("col")
    local_experts = w_gate.shape[0]
    experts = local_experts * owners
    slot_cap = 3 * tok_count * top_count // (2 * experts)
    half_width = width // cols
    pair_count = tok_count * top_count
    rows_per_owner = local_experts * slot_cap
    slots = experts * slot_cap

    flat_routes = routes.reshape(-1)
    expert_ids = jnp.arange(experts, dtype=jnp.int32)
    onehot = (flat_routes[:, None] == expert_ids[None, :]).astype(jnp.int32)
    before = jnp.cumsum(onehot, axis=0) - onehot
    slot_index = jnp.sum(before * onehot, axis=1)
    flat_index = flat_routes * slot_cap + slot_index

    slot_ids = jnp.arange(slots, dtype=jnp.int32)
    match = flat_index.reshape(tok_count, top_count)[:, :, None] == slot_ids[None, None, :]
    weight = jnp.sum(jnp.where(match, probs[:, :, None], 0.0), axis=1)
    taken = jnp.any(match, axis=1)
    picker = taken.astype(jnp.bfloat16)
    weight_hi = weight.astype(jnp.bfloat16)
    weight_lo = (weight - weight_hi.astype(jnp.float32)).astype(jnp.bfloat16)
    prob_of_slot = jnp.sum(weight, axis=0)

    both = ("dp", "col")

    col_me = lax.axis_index("col")
    cot_other = lax.ppermute(cotangent, "col", perm=[(0, 1), (1, 0)])
    cot_full = jnp.where(
        col_me == 0,
        jnp.concatenate([cotangent, cot_other], axis=1),
        jnp.concatenate([cot_other, cotangent], axis=1),
    )

    tok_rows = jnp.einsum("ts,td->sd", picker, tokens, preferred_element_type=jnp.float32)
    cot_rows = jnp.einsum("ts,td->sd", picker, cot_full, preferred_element_type=jnp.float32)
    send = jnp.concatenate(
        [tok_rows.astype(jnp.bfloat16), (prob_of_slot[:, None] * cot_rows).astype(jnp.bfloat16)],
        axis=1,
    )
    arrived = lax.all_to_all(
        send.reshape(owners, rows_per_owner, 2 * width), "dp", 0, 0, tiled=True
    )
    row_block = arrived[:, :, :width]
    d_out = arrived[:, :, width:]

    expert_of_row = jnp.arange(rows_per_owner, dtype=jnp.int32) // slot_cap
    own = (expert_of_row[:, None] == jnp.arange(local_experts, dtype=jnp.int32)[None, :])[
        None, :, :, None
    ]

    def per_half(table):
        return jnp.broadcast_to(
            table.reshape(tok_count, owners, 1, rows_per_owner),
            (tok_count, owners, cols, rows_per_owner),
        )

    def send_back(halves):
        part = jnp.stack([h.astype(jnp.bfloat16) for h in halves], axis=1)
        got = lax.all_to_all(
            part.reshape(owners * cols, rows_per_owner, half_width), both, 0, 0, tiled=True
        )
        return got.reshape(owners, cols, rows_per_owner, half_width)

    def combine(table, got):
        return jnp.einsum("tocr,ocrd->td", per_half(table), got, preferred_element_type=jnp.float32)

    def halves_of(ref, axis):
        return [lax.slice_in_dim(ref, j * half_width, (j + 1) * half_width, axis=axis) for j in range(cols)]

    gate_acts = jnp.einsum("srd,ldh->srlh", row_block, w_gate, preferred_element_type=jnp.float32)
    up_acts = jnp.einsum("srd,ldh->srlh", row_block, w_up, preferred_element_type=jnp.float32)
    gate_acts = jnp.where(own, gate_acts, 0.0)
    up_acts = jnp.where(own, up_acts, 0.0)
    sigmoid_g = jax.nn.sigmoid(gate_acts)
    silu_g = gate_acts * sigmoid_g
    hidden = (silu_g * up_acts).astype(jnp.bfloat16)
    got_out = send_back(
        [
            jnp.einsum("srlh,lhd->srd", hidden, w, preferred_element_type=jnp.float32)
            for w in halves_of(w_down, 2)
        ]
    )
    mixed = (combine(weight_hi, got_out) + combine(weight_lo, got_out)).astype(jnp.bfloat16)
    dots = jnp.einsum("td,ocrd->tocr", cotangent, got_out, preferred_element_type=jnp.float32)
    dots = jnp.sum(dots, axis=2).reshape(tok_count, 1, slots)
    prob_part = jnp.sum(jnp.where(match, dots, 0.0), axis=2)

    grad_down = jnp.einsum(
        "srlh,srd->lhd", hidden, d_out, preferred_element_type=jnp.float32
    ).astype(jnp.bfloat16)
    d_hidden = jnp.einsum("srd,lhd->srlh", d_out, w_down, preferred_element_type=jnp.float32)
    d_hidden = jnp.where(own, d_hidden, 0.0)
    d_gate = (d_hidden * up_acts * sigmoid_g * (1.0 + gate_acts * (1.0 - sigmoid_g))).astype(
        jnp.bfloat16
    )
    d_up = (d_hidden * silu_g).astype(jnp.bfloat16)
    grad_gate = jnp.einsum(
        "srd,srlh->ldh", row_block, d_gate, preferred_element_type=jnp.float32
    ).astype(jnp.bfloat16)
    grad_up = jnp.einsum(
        "srd,srlh->ldh", row_block, d_up, preferred_element_type=jnp.float32
    ).astype(jnp.bfloat16)
    got_grad = send_back(
        [
            jnp.einsum("srlh,ldh->srd", d_gate, wg, preferred_element_type=jnp.float32)
            + jnp.einsum("srlh,ldh->srd", d_up, wu, preferred_element_type=jnp.float32)
            for wg, wu in zip(halves_of(w_gate, 1), halves_of(w_up, 1))
        ]
    )
    grad_tokens = combine(picker, got_grad).astype(jnp.bfloat16)
    grad_probs = lax.psum(prob_part, "col")
    return (mixed, grad_tokens, grad_probs, grad_gate, grad_up, grad_down)


def solution(mesh):
    return jax.shard_map(
        body,
        mesh=mesh,
        in_specs=(
            P("dp", None),
            P("dp", None),
            P("dp", None),
            P("dp", None, "col"),
            P("dp", None, "col"),
            P("dp", "col", None),
            P("dp", "col"),
        ),
        out_specs=(
            P("dp", "col"),
            P("dp", "col"),
            P("dp", None),
            P("dp", None, "col"),
            P("dp", None, "col"),
            P("dp", "col", None),
        ),
        check_vma=False,
    )
```

```python
import jax
import jax.numpy as jnp
from jax import lax
from jax.sharding import PartitionSpec as P


def body(tokens, routes, probs, w_gate, w_up, w_down, cotangent):
    tok_count, width = tokens.shape
    top_count = routes.shape[1]
    owners = lax.axis_size("dp")
    cols = lax.axis_size("col")
    local_experts = w_gate.shape[0]
    experts = local_experts * owners
    slot_cap = 3 * tok_count * top_count // (2 * experts)
    half_width = width // cols
    pair_count = tok_count * top_count
    rows_per_owner = local_experts * slot_cap
    slots = experts * slot_cap

    flat_routes = routes.reshape(-1)
    expert_ids = jnp.arange(experts, dtype=jnp.int32)
    onehot = (flat_routes[:, None] == expert_ids[None, :]).astype(jnp.int32)
    before = jnp.cumsum(onehot, axis=0) - onehot
    slot_index = jnp.sum(before * onehot, axis=1)
    flat_index = flat_routes * slot_cap + slot_index

    slot_ids = jnp.arange(slots, dtype=jnp.int32)
    match = flat_index.reshape(tok_count, top_count)[:, :, None] == slot_ids[None, None, :]
    weight = jnp.sum(jnp.where(match, probs[:, :, None], 0.0), axis=1)
    taken = jnp.any(match, axis=1)
    picker = taken.astype(jnp.bfloat16)
    weight_hi = weight.astype(jnp.bfloat16)
    weight_lo = (weight - weight_hi.astype(jnp.float32)).astype(jnp.bfloat16)
    prob_of_slot = jnp.sum(weight, axis=0)

    both = ("dp", "col")

    col_me = lax.axis_index("col")
    cot_other = lax.ppermute(cotangent, "col", perm=[(0, 1), (1, 0)])
    cot_full = jnp.where(
        col_me == 0,
        jnp.concatenate([cotangent, cot_other], axis=1),
        jnp.concatenate([cot_other, cotangent], axis=1),
    )

    tok_rows = jnp.einsum("ts,td->sd", picker, tokens, preferred_element_type=jnp.float32)
    cot_rows = jnp.einsum("ts,td->sd", picker, cot_full, preferred_element_type=jnp.float32)
    send = jnp.concatenate(
        [tok_rows.astype(jnp.bfloat16), (prob_of_slot[:, None] * cot_rows).astype(jnp.bfloat16)],
        axis=1,
    )
    arrived = lax.all_to_all(
        send.reshape(owners, rows_per_owner, 2 * width), "dp", 0, 0, tiled=True
    )
    row_block = arrived[:, :, :width]
    d_out = arrived[:, :, width:]

    expert_of_row = jnp.arange(rows_per_owner, dtype=jnp.int32) // slot_cap
    own = (expert_of_row[:, None] == jnp.arange(local_experts, dtype=jnp.int32)[None, :])[
        None, :, :, None
    ]

    def per_half(table):
        return jnp.broadcast_to(
            table.reshape(tok_count, owners, 1, rows_per_owner),
            (tok_count, owners, cols, rows_per_owner),
        )

    def send_back(halves):
        part = jnp.stack([h.astype(jnp.bfloat16) for h in halves], axis=1)
        got = lax.all_to_all(
            part.reshape(owners * cols, rows_per_owner, half_width), both, 0, 0, tiled=True
        )
        return got.reshape(owners, cols, rows_per_owner, half_width)

    def combine(table, got):
        return jnp.einsum("tocr,ocrd->td", per_half(table), got, preferred_element_type=jnp.float32)

    def halves_of(ref, axis):
        return [lax.slice_in_dim(ref, j * half_width, (j + 1) * half_width, axis=axis) for j in range(cols)]

    gate_acts = jnp.einsum("srd,ldh->srlh", row_block, w_gate, preferred_element_type=jnp.float32)
    up_acts = jnp.einsum("srd,ldh->srlh", row_block, w_up, preferred_element_type=jnp.float32)
    gate_acts = jnp.where(own, gate_acts, 0.0)
    up_acts = jnp.where(own, up_acts, 0.0)
    sigmoid_g = jax.nn.sigmoid(gate_acts)
    silu_g = gate_acts * sigmoid_g
    hidden = (silu_g * up_acts).astype(jnp.bfloat16)
    got_out = send_back(
        [
            jnp.einsum("srlh,lhd->srd", hidden, w, preferred_element_type=jnp.float32)
            for w in halves_of(w_down, 2)
        ]
    )
    stacked = jnp.broadcast_to(
        jnp.stack([weight_hi, weight_lo]).reshape(2, tok_count, owners, 1, rows_per_owner),
        (2, tok_count, owners, cols, rows_per_owner),
    )
    both_parts = jnp.einsum("utocr,ocrd->utd", stacked, got_out, preferred_element_type=jnp.float32)
    mixed = (both_parts[0] + both_parts[1]).astype(jnp.bfloat16)
    dots = jnp.einsum("td,ocrd->tocr", cotangent, got_out, preferred_element_type=jnp.float32)
    dots = jnp.sum(dots, axis=2).reshape(tok_count, 1, slots)
    prob_part = jnp.sum(jnp.where(match, dots, 0.0), axis=2)

    grad_down = jnp.einsum(
        "srlh,srd->lhd", hidden, d_out, preferred_element_type=jnp.float32
    ).astype(jnp.bfloat16)
    d_hidden = jnp.einsum("srd,lhd->srlh", d_out, w_down, preferred_element_type=jnp.float32)
    d_hidden = jnp.where(own, d_hidden, 0.0)
    d_gate = (d_hidden * up_acts * sigmoid_g * (1.0 + gate_acts * (1.0 - sigmoid_g))).astype(
        jnp.bfloat16
    )
    d_up = (d_hidden * silu_g).astype(jnp.bfloat16)
    grad_gate = jnp.einsum(
        "srd,srlh->ldh", row_block, d_gate, preferred_element_type=jnp.float32
    ).astype(jnp.bfloat16)
    grad_up = jnp.einsum(
        "srd,srlh->ldh", row_block, d_up, preferred_element_type=jnp.float32
    ).astype(jnp.bfloat16)
    got_grad = send_back(
        [
            jnp.einsum("srlh,ldh->srd", d_gate, wg, preferred_element_type=jnp.float32)
            + jnp.einsum("srlh,ldh->srd", d_up, wu, preferred_element_type=jnp.float32)
            for wg, wu in zip(halves_of(w_gate, 1), halves_of(w_up, 1))
        ]
    )
    grad_tokens = combine(picker, got_grad).astype(jnp.bfloat16)
    prob_part, mixed = lax.optimization_barrier((prob_part, mixed))
    grad_probs = lax.psum(prob_part, "col")
    return (mixed, grad_tokens, grad_probs, grad_gate, grad_up, grad_down)


def solution(mesh):
    return jax.shard_map(
        body,
        mesh=mesh,
        in_specs=(
            P("dp", None),
            P("dp", None),
            P("dp", None),
            P("dp", None, "col"),
            P("dp", None, "col"),
            P("dp", "col", None),
            P("dp", "col"),
        ),
        out_specs=(
            P("dp", "col"),
            P("dp", "col"),
            P("dp", None),
            P("dp", None, "col"),
            P("dp", None, "col"),
            P("dp", "col", None),
        ),
        check_vma=False,
    )
```

```python
import jax
import jax.numpy as jnp
from jax import lax
from jax.sharding import PartitionSpec as P


def body(tokens, routes, probs, w_gate, w_up, w_down, cotangent):
    tok_count, width = tokens.shape
    top_count = routes.shape[1]
    owners = lax.axis_size("dp")
    cols = lax.axis_size("col")
    local_experts = w_gate.shape[0]
    experts = local_experts * owners
    slot_cap = 3 * tok_count * top_count // (2 * experts)
    half_width = width // cols
    pair_count = tok_count * top_count
    rows_per_owner = local_experts * slot_cap
    slots = experts * slot_cap

    flat_routes = routes.reshape(-1)
    expert_ids = jnp.arange(experts, dtype=jnp.int32)
    onehot = (flat_routes[:, None] == expert_ids[None, :]).astype(jnp.int32)
    before = jnp.cumsum(onehot, axis=0) - onehot
    slot_index = jnp.sum(before * onehot, axis=1)
    flat_index = flat_routes * slot_cap + slot_index

    slot_ids = jnp.arange(slots, dtype=jnp.int32)
    match = flat_index.reshape(tok_count, top_count)[:, :, None] == slot_ids[None, None, :]
    weight = jnp.sum(jnp.where(match, probs[:, :, None], 0.0), axis=1)
    taken = jnp.any(match, axis=1)
    picker = taken.astype(jnp.bfloat16)
    weight_hi = weight.astype(jnp.bfloat16)
    weight_lo = (weight - weight_hi.astype(jnp.float32)).astype(jnp.bfloat16)
    prob_of_slot = jnp.sum(weight, axis=0)

    both = ("dp", "col")

    col_me = lax.axis_index("col")
    cot_other = lax.ppermute(cotangent, "col", perm=[(0, 1), (1, 0)])
    cot_full = jnp.where(
        col_me == 0,
        jnp.concatenate([cotangent, cot_other], axis=1),
        jnp.concatenate([cot_other, cotangent], axis=1),
    )

    tok_rows = jnp.einsum("ts,td->sd", picker, tokens, preferred_element_type=jnp.float32)
    cot_rows = jnp.einsum("ts,td->sd", picker, cot_full, preferred_element_type=jnp.float32)
    send_tok = tok_rows.astype(jnp.bfloat16).reshape(owners, rows_per_owner, width)
    row_block = lax.all_to_all(send_tok, "dp", 0, 0, tiled=True)
    send_cot = (prob_of_slot[:, None] * cot_rows).astype(jnp.bfloat16)
    d_out = lax.all_to_all(
        send_cot.reshape(owners, rows_per_owner, width), "dp", 0, 0, tiled=True
    )

    expert_of_row = jnp.arange(rows_per_owner, dtype=jnp.int32) // slot_cap
    own = (expert_of_row[:, None] == jnp.arange(local_experts, dtype=jnp.int32)[None, :])[
        None, :, :, None
    ]

    def per_half(table):
        return jnp.broadcast_to(
            table.reshape(tok_count, owners, 1, rows_per_owner),
            (tok_count, owners, cols, rows_per_owner),
        )

    def send_back(halves):
        part = jnp.stack([h.astype(jnp.bfloat16) for h in halves], axis=1)
        got = lax.all_to_all(
            part.reshape(owners * cols, rows_per_owner, half_width), both, 0, 0, tiled=True
        )
        return got.reshape(owners, cols, rows_per_owner, half_width)

    def combine(table, got):
        return jnp.einsum("tocr,ocrd->td", per_half(table), got, preferred_element_type=jnp.float32)

    def halves_of(ref, axis):
        return [lax.slice_in_dim(ref, j * half_width, (j + 1) * half_width, axis=axis) for j in range(cols)]

    gate_acts = jnp.einsum("srd,ldh->srlh", row_block, w_gate, preferred_element_type=jnp.float32)
    up_acts = jnp.einsum("srd,ldh->srlh", row_block, w_up, preferred_element_type=jnp.float32)
    gate_acts = jnp.where(own, gate_acts, 0.0)
    up_acts = jnp.where(own, up_acts, 0.0)
    sigmoid_g = jax.nn.sigmoid(gate_acts)
    silu_g = gate_acts * sigmoid_g
    hidden = (silu_g * up_acts).astype(jnp.bfloat16)
    out_halves = [
        jnp.einsum("srlh,lhd->srd", hidden, w, preferred_element_type=jnp.float32)
        for w in halves_of(w_down, 2)
    ]
    d_out, out_halves = lax.optimization_barrier((d_out, out_halves))
    got_out = send_back(out_halves)
    stacked = jnp.broadcast_to(
        jnp.stack([weight_hi, weight_lo]).reshape(2, tok_count, owners, 1, rows_per_owner),
        (2, tok_count, owners, cols, rows_per_owner),
    )
    both_parts = jnp.einsum("utocr,ocrd->utd", stacked, got_out, preferred_element_type=jnp.float32)
    mixed = (both_parts[0] + both_parts[1]).astype(jnp.bfloat16)
    dots = jnp.einsum("td,ocrd->tocr", cotangent, got_out, preferred_element_type=jnp.float32)
    dots = jnp.sum(dots, axis=2).reshape(tok_count, 1, slots)
    prob_part = jnp.sum(jnp.where(match, dots, 0.0), axis=2)

    grad_down = jnp.einsum(
        "srlh,srd->lhd", hidden, d_out, preferred_element_type=jnp.float32
    ).astype(jnp.bfloat16)
    d_hidden = jnp.einsum("srd,lhd->srlh", d_out, w_down, preferred_element_type=jnp.float32)
    d_hidden = jnp.where(own, d_hidden, 0.0)
    d_gate = (d_hidden * up_acts * sigmoid_g * (1.0 + gate_acts * (1.0 - sigmoid_g))).astype(
        jnp.bfloat16
    )
    d_up = (d_hidden * silu_g).astype(jnp.bfloat16)
    grad_gate = jnp.einsum(
        "srd,srlh->ldh", row_block, d_gate, preferred_element_type=jnp.float32
    ).astype(jnp.bfloat16)
    grad_up = jnp.einsum(
        "srd,srlh->ldh", row_block, d_up, preferred_element_type=jnp.float32
    ).astype(jnp.bfloat16)
    got_grad = send_back(
        [
            jnp.einsum("srlh,ldh->srd", d_gate, wg, preferred_element_type=jnp.float32)
            + jnp.einsum("srlh,ldh->srd", d_up, wu, preferred_element_type=jnp.float32)
            for wg, wu in zip(halves_of(w_gate, 1), halves_of(w_up, 1))
        ]
    )
    grad_tokens = combine(picker, got_grad).astype(jnp.bfloat16)
    prob_part, mixed = lax.optimization_barrier((prob_part, mixed))
    grad_probs = lax.psum(prob_part, "col")
    return (mixed, grad_tokens, grad_probs, grad_gate, grad_up, grad_down)


def solution(mesh):
    return jax.shard_map(
        body,
        mesh=mesh,
        in_specs=(
            P("dp", None),
            P("dp", None),
            P("dp", None),
            P("dp", None, "col"),
            P("dp", None, "col"),
            P("dp", "col", None),
            P("dp", "col"),
        ),
        out_specs=(
            P("dp", "col"),
            P("dp", "col"),
            P("dp", None),
            P("dp", None, "col"),
            P("dp", None, "col"),
            P("dp", "col", None),
        ),
        check_vma=False,
    )
```

```python
import jax
import jax.numpy as jnp
from jax import lax
from jax.sharding import PartitionSpec as P


def body(tokens, routes, probs, w_gate, w_up, w_down, cotangent):
    tok_count, width = tokens.shape
    top_count = routes.shape[1]
    owners = lax.axis_size("dp")
    cols = lax.axis_size("col")
    local_experts = w_gate.shape[0]
    experts = local_experts * owners
    slot_cap = 3 * tok_count * top_count // (2 * experts)
    half_width = width // cols
    pair_count = tok_count * top_count
    rows_per_owner = local_experts * slot_cap
    slots = experts * slot_cap

    flat_routes = routes.reshape(-1)
    expert_ids = jnp.arange(experts, dtype=jnp.int32)
    onehot = (flat_routes[:, None] == expert_ids[None, :]).astype(jnp.int32)
    before = jnp.cumsum(onehot, axis=0) - onehot
    slot_index = jnp.sum(before * onehot, axis=1)
    flat_index = flat_routes * slot_cap + slot_index

    slot_ids = jnp.arange(slots, dtype=jnp.int32)
    match = flat_index.reshape(tok_count, top_count)[:, :, None] == slot_ids[None, None, :]
    weight = jnp.sum(jnp.where(match, probs[:, :, None], 0.0), axis=1)
    taken = jnp.any(match, axis=1)
    picker = taken.astype(jnp.bfloat16)
    weight_hi = weight.astype(jnp.bfloat16)
    weight_lo = (weight - weight_hi.astype(jnp.float32)).astype(jnp.bfloat16)
    prob_of_slot = jnp.sum(weight, axis=0)

    both = ("dp", "col")

    col_me = lax.axis_index("col")
    cot_other = lax.ppermute(cotangent, "col", perm=[(0, 1), (1, 0)])
    tok_rows = jnp.einsum("ts,td->sd", picker, tokens, preferred_element_type=jnp.float32)
    cot_full = jnp.where(
        col_me == 0,
        jnp.concatenate([cotangent, cot_other], axis=1),
        jnp.concatenate([cot_other, cotangent], axis=1),
    )

    cot_rows = jnp.einsum("ts,td->sd", picker, cot_full, preferred_element_type=jnp.float32)
    send_tok = tok_rows.astype(jnp.bfloat16).reshape(owners, rows_per_owner, width)
    cot_other, send_tok = lax.optimization_barrier((cot_other, send_tok))
    row_block = lax.all_to_all(send_tok, "dp", 0, 0, tiled=True)
    send_cot = (prob_of_slot[:, None] * cot_rows).astype(jnp.bfloat16)
    d_out = lax.all_to_all(
        send_cot.reshape(owners, rows_per_owner, width), "dp", 0, 0, tiled=True
    )

    expert_of_row = jnp.arange(rows_per_owner, dtype=jnp.int32) // slot_cap
    own = (expert_of_row[:, None] == jnp.arange(local_experts, dtype=jnp.int32)[None, :])[
        None, :, :, None
    ]

    def per_half(table):
        return jnp.broadcast_to(
            table.reshape(tok_count, owners, 1, rows_per_owner),
            (tok_count, owners, cols, rows_per_owner),
        )

    def send_back(halves):
        part = jnp.stack([h.astype(jnp.bfloat16) for h in halves], axis=1)
        got = lax.all_to_all(
            part.reshape(owners * cols, rows_per_owner, half_width), both, 0, 0, tiled=True
        )
        return got.reshape(owners, cols, rows_per_owner, half_width)

    def combine(table, got):
        return jnp.einsum("tocr,ocrd->td", per_half(table), got, preferred_element_type=jnp.float32)

    def halves_of(ref, axis):
        return [lax.slice_in_dim(ref, j * half_width, (j + 1) * half_width, axis=axis) for j in range(cols)]

    gate_acts = jnp.einsum("srd,ldh->srlh", row_block, w_gate, preferred_element_type=jnp.float32)
    up_acts = jnp.einsum("srd,ldh->srlh", row_block, w_up, preferred_element_type=jnp.float32)
    gate_acts = jnp.where(own, gate_acts, 0.0)
    up_acts = jnp.where(own, up_acts, 0.0)
    sigmoid_g = jax.nn.sigmoid(gate_acts)
    silu_g = gate_acts * sigmoid_g
    hidden = (silu_g * up_acts).astype(jnp.bfloat16)
    out_halves = [
        jnp.einsum("srlh,lhd->srd", hidden, w, preferred_element_type=jnp.float32)
        for w in halves_of(w_down, 2)
    ]
    d_out, out_halves = lax.optimization_barrier((d_out, out_halves))
    got_out = send_back(out_halves)
    stacked = jnp.broadcast_to(
        jnp.stack([weight_hi, weight_lo]).reshape(2, tok_count, owners, 1, rows_per_owner),
        (2, tok_count, owners, cols, rows_per_owner),
    )
    both_parts = jnp.einsum("utocr,ocrd->utd", stacked, got_out, preferred_element_type=jnp.float32)
    mixed = (both_parts[0] + both_parts[1]).astype(jnp.bfloat16)
    dots = jnp.einsum("td,ocrd->tocr", cotangent, got_out, preferred_element_type=jnp.float32)
    dots = jnp.sum(dots, axis=2).reshape(tok_count, 1, slots)
    prob_part = jnp.sum(jnp.where(match, dots, 0.0), axis=2)

    grad_down = jnp.einsum(
        "srlh,srd->lhd", hidden, d_out, preferred_element_type=jnp.float32
    ).astype(jnp.bfloat16)
    d_hidden = jnp.einsum("srd,lhd->srlh", d_out, w_down, preferred_element_type=jnp.float32)
    d_hidden = jnp.where(own, d_hidden, 0.0)
    d_gate = (d_hidden * up_acts * sigmoid_g * (1.0 + gate_acts * (1.0 - sigmoid_g))).astype(
        jnp.bfloat16
    )
    d_up = (d_hidden * silu_g).astype(jnp.bfloat16)
    grad_gate = jnp.einsum(
        "srd,srlh->ldh", row_block, d_gate, preferred_element_type=jnp.float32
    ).astype(jnp.bfloat16)
    grad_up = jnp.einsum(
        "srd,srlh->ldh", row_block, d_up, preferred_element_type=jnp.float32
    ).astype(jnp.bfloat16)
    got_grad = send_back(
        [
            jnp.einsum("srlh,ldh->srd", d_gate, wg, preferred_element_type=jnp.float32)
            + jnp.einsum("srlh,ldh->srd", d_up, wu, preferred_element_type=jnp.float32)
            for wg, wu in zip(halves_of(w_gate, 1), halves_of(w_up, 1))
        ]
    )
    grad_tokens = combine(picker, got_grad).astype(jnp.bfloat16)
    prob_part, mixed = lax.optimization_barrier((prob_part, mixed))
    grad_probs = lax.psum(prob_part, "col")
    return (mixed, grad_tokens, grad_probs, grad_gate, grad_up, grad_down)


def solution(mesh):
    return jax.shard_map(
        body,
        mesh=mesh,
        in_specs=(
            P("dp", None),
            P("dp", None),
            P("dp", None),
            P("dp", None, "col"),
            P("dp", None, "col"),
            P("dp", "col", None),
            P("dp", "col"),
        ),
        out_specs=(
            P("dp", "col"),
            P("dp", "col"),
            P("dp", None),
            P("dp", None, "col"),
            P("dp", None, "col"),
            P("dp", "col", None),
        ),
        check_vma=False,
    )
```

```python
import jax
import jax.numpy as jnp
from jax import lax
from jax.sharding import PartitionSpec as P


def body(tokens, routes, probs, w_gate, w_up, w_down, cotangent):
    tok_count, width = tokens.shape
    top_count = routes.shape[1]
    owners = lax.axis_size("dp")
    cols = lax.axis_size("col")
    local_experts = w_gate.shape[0]
    experts = local_experts * owners
    slot_cap = 3 * tok_count * top_count // (2 * experts)
    half_width = width // cols
    pair_count = tok_count * top_count
    rows_per_owner = local_experts * slot_cap
    slots = experts * slot_cap

    flat_routes = routes.reshape(-1)
    expert_ids = jnp.arange(experts, dtype=jnp.int32)
    onehot = (flat_routes[:, None] == expert_ids[None, :]).astype(jnp.int32)
    before = jnp.cumsum(onehot, axis=0) - onehot
    slot_index = jnp.sum(before * onehot, axis=1)
    flat_index = flat_routes * slot_cap + slot_index

    slot_ids = jnp.arange(slots, dtype=jnp.int32)
    match = flat_index.reshape(tok_count, top_count)[:, :, None] == slot_ids[None, None, :]
    weight = jnp.sum(jnp.where(match, probs[:, :, None], 0.0), axis=1)
    taken = jnp.any(match, axis=1)
    picker = taken.astype(jnp.bfloat16)
    weight_hi = weight.astype(jnp.bfloat16)
    weight_lo = (weight - weight_hi.astype(jnp.float32)).astype(jnp.bfloat16)
    prob_of_slot = jnp.sum(weight, axis=0)

    both = ("dp", "col")

    col_me = lax.axis_index("col")
    cot_other = lax.ppermute(cotangent, "col", perm=[(0, 1), (1, 0)])
    tok_rows = jnp.einsum("ts,td->sd", picker, tokens, preferred_element_type=jnp.float32)
    cot_full = jnp.where(
        col_me == 0,
        jnp.concatenate([cotangent, cot_other], axis=1),
        jnp.concatenate([cot_other, cotangent], axis=1),
    )

    cot_rows = jnp.einsum("ts,td->sd", picker, cot_full, preferred_element_type=jnp.float32)
    send_tok = tok_rows.astype(jnp.bfloat16).reshape(owners, rows_per_owner, width)
    cot_other, send_tok = lax.optimization_barrier((cot_other, send_tok))
    row_block = lax.all_to_all(send_tok, "dp", 0, 0, tiled=True)
    send_cot = (prob_of_slot[:, None] * cot_rows).astype(jnp.bfloat16)
    d_out = lax.all_to_all(
        send_cot.reshape(owners, rows_per_owner, width), "dp", 0, 0, tiled=True
    )

    expert_of_row = jnp.arange(rows_per_owner, dtype=jnp.int32) // slot_cap
    own = (expert_of_row[:, None] == jnp.arange(local_experts, dtype=jnp.int32)[None, :])[
        None, :, :, None
    ]

    def per_half(table):
        return jnp.broadcast_to(
            table.reshape(tok_count, owners, 1, rows_per_owner),
            (tok_count, owners, cols, rows_per_owner),
        )

    def send_back(halves):
        part = jnp.stack([h.astype(jnp.bfloat16) for h in halves], axis=1)
        got = lax.all_to_all(
            part.reshape(owners * cols, rows_per_owner, half_width), both, 0, 0, tiled=True
        )
        return got.reshape(owners, cols, rows_per_owner, half_width)

    def flat(got):
        return got.reshape(owners * cols * rows_per_owner, half_width)

    def combine(table, got):
        lhs = per_half(table).reshape(tok_count, owners * cols * rows_per_owner)
        return jnp.dot(lhs, flat(got), preferred_element_type=jnp.float32)

    def halves_of(ref, axis):
        return [lax.slice_in_dim(ref, j * half_width, (j + 1) * half_width, axis=axis) for j in range(cols)]

    gate_acts = jnp.einsum("srd,ldh->srlh", row_block, w_gate, preferred_element_type=jnp.float32)
    up_acts = jnp.einsum("srd,ldh->srlh", row_block, w_up, preferred_element_type=jnp.float32)
    gate_acts = jnp.where(own, gate_acts, 0.0)
    up_acts = jnp.where(own, up_acts, 0.0)
    sigmoid_g = jax.nn.sigmoid(gate_acts)
    silu_g = gate_acts * sigmoid_g
    hidden = (silu_g * up_acts).astype(jnp.bfloat16)
    out_halves = [
        jnp.einsum("srlh,lhd->srd", hidden, w, preferred_element_type=jnp.float32)
        for w in halves_of(w_down, 2)
    ]
    d_out, out_halves = lax.optimization_barrier((d_out, out_halves))
    got_out = send_back(out_halves)
    stacked = jnp.broadcast_to(
        jnp.stack([weight_hi, weight_lo]).reshape(2, tok_count, owners, 1, rows_per_owner),
        (2, tok_count, owners, cols, rows_per_owner),
    )
    both_parts = jnp.dot(
        stacked.reshape(2 * tok_count, owners * cols * rows_per_owner),
        flat(got_out),
        preferred_element_type=jnp.float32,
    )
    mixed = (both_parts[:tok_count] + both_parts[tok_count:]).astype(jnp.bfloat16)
    dots = lax.dot_general(
        cotangent, flat(got_out), (((1,), (1,)), ((), ())), preferred_element_type=jnp.float32
    ).reshape(tok_count, owners, cols, rows_per_owner)
    dots = jnp.sum(dots, axis=2).reshape(tok_count, 1, slots)
    prob_part = jnp.sum(jnp.where(match, dots, 0.0), axis=2)

    grad_down = jnp.einsum(
        "srlh,srd->lhd", hidden, d_out, preferred_element_type=jnp.float32
    ).astype(jnp.bfloat16)
    d_hidden = jnp.einsum("srd,lhd->srlh", d_out, w_down, preferred_element_type=jnp.float32)
    d_hidden = jnp.where(own, d_hidden, 0.0)
    d_gate = (d_hidden * up_acts * sigmoid_g * (1.0 + gate_acts * (1.0 - sigmoid_g))).astype(
        jnp.bfloat16
    )
    d_up = (d_hidden * silu_g).astype(jnp.bfloat16)
    grad_gate = jnp.einsum(
        "srd,srlh->ldh", row_block, d_gate, preferred_element_type=jnp.float32
    ).astype(jnp.bfloat16)
    grad_up = jnp.einsum(
        "srd,srlh->ldh", row_block, d_up, preferred_element_type=jnp.float32
    ).astype(jnp.bfloat16)
    got_grad = send_back(
        [
            jnp.einsum("srlh,ldh->srd", d_gate, wg, preferred_element_type=jnp.float32)
            + jnp.einsum("srlh,ldh->srd", d_up, wu, preferred_element_type=jnp.float32)
            for wg, wu in zip(halves_of(w_gate, 1), halves_of(w_up, 1))
        ]
    )
    grad_tokens = combine(picker, got_grad).astype(jnp.bfloat16)
    prob_part, mixed = lax.optimization_barrier((prob_part, mixed))
    grad_probs = lax.psum(prob_part, "col")
    return (mixed, grad_tokens, grad_probs, grad_gate, grad_up, grad_down)


def solution(mesh):
    return jax.shard_map(
        body,
        mesh=mesh,
        in_specs=(
            P("dp", None),
            P("dp", None),
            P("dp", None),
            P("dp", None, "col"),
            P("dp", None, "col"),
            P("dp", "col", None),
            P("dp", "col"),
        ),
        out_specs=(
            P("dp", "col"),
            P("dp", "col"),
            P("dp", None),
            P("dp", None, "col"),
            P("dp", None, "col"),
            P("dp", "col", None),
        ),
        check_vma=False,
    )
```

```python
import jax
import jax.numpy as jnp
from jax import lax
from jax.sharding import PartitionSpec as P


def body(tokens, routes, probs, w_gate, w_up, w_down, cotangent):
    tok_count, width = tokens.shape
    top_count = routes.shape[1]
    owners = lax.axis_size("dp")
    cols = lax.axis_size("col")
    local_experts = w_gate.shape[0]
    experts = local_experts * owners
    slot_cap = 3 * tok_count * top_count // (2 * experts)
    half_width = width // cols
    pair_count = tok_count * top_count
    rows_per_owner = local_experts * slot_cap
    slots = experts * slot_cap

    flat_routes = routes.reshape(-1)
    expert_ids = jnp.arange(experts, dtype=jnp.int32)
    onehot = (flat_routes[:, None] == expert_ids[None, :]).astype(jnp.int32)
    before = jnp.cumsum(onehot, axis=0) - onehot
    slot_index = jnp.sum(before * onehot, axis=1)
    flat_index = flat_routes * slot_cap + slot_index

    slot_ids = jnp.arange(slots, dtype=jnp.int32)
    match = flat_index.reshape(tok_count, top_count)[:, :, None] == slot_ids[None, None, :]
    weight = jnp.sum(jnp.where(match, probs[:, :, None], 0.0), axis=1)
    taken = jnp.any(match, axis=1)
    picker = taken.astype(jnp.bfloat16)
    weight_hi = weight.astype(jnp.bfloat16)
    weight_lo = (weight - weight_hi.astype(jnp.float32)).astype(jnp.bfloat16)
    prob_of_slot = jnp.sum(weight, axis=0)

    both = ("dp", "col")

    col_me = lax.axis_index("col")
    cot_other = lax.ppermute(cotangent, "col", perm=[(0, 1), (1, 0)])
    tok_rows = jnp.einsum("ts,td->sd", picker, tokens, preferred_element_type=jnp.float32)
    cot_full = jnp.where(
        col_me == 0,
        jnp.concatenate([cotangent, cot_other], axis=1),
        jnp.concatenate([cot_other, cotangent], axis=1),
    )

    cot_rows = jnp.einsum("ts,td->sd", picker, cot_full, preferred_element_type=jnp.float32)
    send_tok = tok_rows.astype(jnp.bfloat16).reshape(owners, rows_per_owner, width)
    cot_other, send_tok = lax.optimization_barrier((cot_other, send_tok))
    row_block = lax.all_to_all(send_tok, "dp", 0, 0, tiled=True)
    send_cot = (prob_of_slot[:, None] * cot_rows).astype(jnp.bfloat16)
    d_out = lax.all_to_all(
        send_cot.reshape(owners, rows_per_owner, width), "dp", 0, 0, tiled=True
    )

    expert_of_row = jnp.arange(rows_per_owner, dtype=jnp.int32) // slot_cap
    own = (expert_of_row[:, None] == jnp.arange(local_experts, dtype=jnp.int32)[None, :])[
        None, :, :, None
    ]

    def per_half(table):
        return jnp.broadcast_to(
            table.reshape(tok_count, owners, 1, rows_per_owner),
            (tok_count, owners, cols, rows_per_owner),
        )

    def send_back(halves):
        part = jnp.stack([h.astype(jnp.bfloat16) for h in halves], axis=1)
        got = lax.all_to_all(
            part.reshape(owners * cols, rows_per_owner, half_width), both, 0, 0, tiled=True
        )
        return got.reshape(owners, cols, rows_per_owner, half_width)

    def flat(got):
        return got.reshape(owners * cols * rows_per_owner, half_width)

    def combine(table, got):
        lhs = per_half(table).reshape(tok_count, owners * cols * rows_per_owner)
        return jnp.dot(lhs, flat(got), preferred_element_type=jnp.float32)

    def halves_of(ref, axis):
        return [lax.slice_in_dim(ref, j * half_width, (j + 1) * half_width, axis=axis) for j in range(cols)]

    gate_acts = jnp.einsum("srd,ldh->srlh", row_block, w_gate, preferred_element_type=jnp.float32)
    up_acts = jnp.einsum("srd,ldh->srlh", row_block, w_up, preferred_element_type=jnp.float32)
    gate_acts = jnp.where(own, gate_acts, 0.0)
    up_acts = jnp.where(own, up_acts, 0.0)
    sigmoid_g = jax.nn.sigmoid(gate_acts)
    silu_g = gate_acts * sigmoid_g
    hidden = (silu_g * up_acts).astype(jnp.bfloat16)
    out_halves = [
        jnp.einsum("srlh,lhd->srd", hidden, w, preferred_element_type=jnp.float32)
        for w in halves_of(w_down, 2)
    ]
    d_out, out_halves = lax.optimization_barrier((d_out, out_halves))
    got_out = send_back(out_halves)
    stacked = jnp.broadcast_to(
        jnp.stack([weight_hi, weight_lo]).reshape(2, tok_count, owners, 1, rows_per_owner),
        (2, tok_count, owners, cols, rows_per_owner),
    )
    both_parts = jnp.dot(
        stacked.reshape(2 * tok_count, owners * cols * rows_per_owner),
        flat(got_out),
        preferred_element_type=jnp.float32,
    )
    mixed = (both_parts[:tok_count] + both_parts[tok_count:]).astype(jnp.bfloat16)
    dots = lax.dot_general(
        cotangent, flat(got_out), (((1,), (1,)), ((), ())), preferred_element_type=jnp.float32
    ).reshape(tok_count, owners, cols, rows_per_owner)
    dots = jnp.sum(dots, axis=2).reshape(tok_count, 1, slots)
    prob_part = jnp.sum(jnp.where(match, dots, 0.0), axis=2)

    grad_down = jnp.einsum(
        "srlh,srd->lhd", hidden, d_out, preferred_element_type=jnp.float32
    ).astype(jnp.bfloat16)
    d_hidden = jnp.einsum("srd,lhd->srlh", d_out, w_down, preferred_element_type=jnp.float32)
    d_hidden = jnp.where(own, d_hidden, 0.0)
    d_gate = (d_hidden * up_acts * sigmoid_g * (1.0 + gate_acts * (1.0 - sigmoid_g))).astype(
        jnp.bfloat16
    )
    d_up = (d_hidden * silu_g).astype(jnp.bfloat16)
    grad_gate = jnp.einsum(
        "srd,srlh->ldh", row_block, d_gate, preferred_element_type=jnp.float32
    ).astype(jnp.bfloat16)
    grad_up = jnp.einsum(
        "srd,srlh->ldh", row_block, d_up, preferred_element_type=jnp.float32
    ).astype(jnp.bfloat16)
    row_halves = [
        jnp.einsum("srlh,ldh->srd", d_gate, wg, preferred_element_type=jnp.float32)
        + jnp.einsum("srlh,ldh->srd", d_up, wu, preferred_element_type=jnp.float32)
        for wg, wu in zip(halves_of(w_gate, 1), halves_of(w_up, 1))
    ]
    grad_down, row_halves = lax.optimization_barrier((grad_down, row_halves))
    got_grad = send_back(row_halves)
    grad_tokens = combine(picker, got_grad).astype(jnp.bfloat16)
    prob_part, mixed = lax.optimization_barrier((prob_part, mixed))
    grad_probs = lax.psum(prob_part, "col")
    return (mixed, grad_tokens, grad_probs, grad_gate, grad_up, grad_down)


def solution(mesh):
    return jax.shard_map(
        body,
        mesh=mesh,
        in_specs=(
            P("dp", None),
            P("dp", None),
            P("dp", None),
            P("dp", None, "col"),
            P("dp", None, "col"),
            P("dp", "col", None),
            P("dp", "col"),
        ),
        out_specs=(
            P("dp", "col"),
            P("dp", "col"),
            P("dp", None),
            P("dp", None, "col"),
            P("dp", None, "col"),
            P("dp", "col", None),
        ),
        check_vma=False,
    )
```

```python
import jax
import jax.numpy as jnp
from jax import lax
from jax.sharding import PartitionSpec as P


def body(tokens, routes, probs, w_gate, w_up, w_down, cotangent):
    tok_count, width = tokens.shape
    top_count = routes.shape[1]
    owners = lax.axis_size("dp")
    cols = lax.axis_size("col")
    local_experts = w_gate.shape[0]
    experts = local_experts * owners
    slot_cap = 3 * tok_count * top_count // (2 * experts)
    half_width = width // cols
    pair_count = tok_count * top_count
    rows_per_owner = local_experts * slot_cap
    slots = experts * slot_cap

    flat_routes = routes.reshape(-1)
    expert_ids = jnp.arange(experts, dtype=jnp.int32)
    onehot = (flat_routes[:, None] == expert_ids[None, :]).astype(jnp.int32)
    before = jnp.cumsum(onehot, axis=0) - onehot
    slot_index = jnp.sum(before * onehot, axis=1)
    flat_index = flat_routes * slot_cap + slot_index

    slot_ids = jnp.arange(slots, dtype=jnp.int32)
    match = flat_index.reshape(tok_count, top_count)[:, :, None] == slot_ids[None, None, :]
    weight = jnp.sum(jnp.where(match, probs[:, :, None], 0.0), axis=1)
    taken = jnp.any(match, axis=1)
    picker = taken.astype(jnp.bfloat16)
    weight_hi = weight.astype(jnp.bfloat16)
    weight_lo = (weight - weight_hi.astype(jnp.float32)).astype(jnp.bfloat16)
    prob_of_slot = jnp.sum(weight, axis=0)

    both = ("dp", "col")

    col_me = lax.axis_index("col")
    tok_half = lax.dynamic_slice_in_dim(tokens, col_me * half_width, half_width, axis=1)
    tok_rows = jnp.einsum("ts,td->sd", picker, tok_half, preferred_element_type=jnp.float32)
    cot_rows = jnp.einsum("ts,td->sd", picker, cotangent, preferred_element_type=jnp.float32)

    def dispatch(rows_half):
        spread = jnp.broadcast_to(
            rows_half.reshape(owners, 1, rows_per_owner, half_width),
            (owners, cols, rows_per_owner, half_width),
        ).reshape(owners * cols, rows_per_owner, half_width)
        got = lax.all_to_all(spread, both, 0, 0, tiled=True)
        return got.reshape(owners, cols, rows_per_owner, half_width)

    row_block = dispatch(tok_rows.astype(jnp.bfloat16))
    d_out = dispatch((prob_of_slot[:, None] * cot_rows).astype(jnp.bfloat16))
    w_gate_h = w_gate.reshape(local_experts, cols, half_width, -1)
    w_up_h = w_up.reshape(local_experts, cols, half_width, -1)
    w_down_h = w_down.reshape(local_experts, w_down.shape[1], cols, half_width)

    expert_of_row = jnp.arange(rows_per_owner, dtype=jnp.int32) // slot_cap
    own = (expert_of_row[:, None] == jnp.arange(local_experts, dtype=jnp.int32)[None, :])[
        None, :, :, None
    ]

    def per_half(table):
        return jnp.broadcast_to(
            table.reshape(tok_count, owners, 1, rows_per_owner),
            (tok_count, owners, cols, rows_per_owner),
        )

    def send_back(halves):
        part = jnp.stack([h.astype(jnp.bfloat16) for h in halves], axis=1)
        got = lax.all_to_all(
            part.reshape(owners * cols, rows_per_owner, half_width), both, 0, 0, tiled=True
        )
        return got.reshape(owners, cols, rows_per_owner, half_width)

    def flat(got):
        return got.reshape(owners * cols * rows_per_owner, half_width)

    def combine(table, got):
        lhs = per_half(table).reshape(tok_count, owners * cols * rows_per_owner)
        return jnp.dot(lhs, flat(got), preferred_element_type=jnp.float32)

    def halves_of(ref, axis):
        return [lax.slice_in_dim(ref, j * half_width, (j + 1) * half_width, axis=axis) for j in range(cols)]

    gate_acts = jnp.einsum("scrd,lcdh->srlh", row_block, w_gate_h, preferred_element_type=jnp.float32)
    up_acts = jnp.einsum("scrd,lcdh->srlh", row_block, w_up_h, preferred_element_type=jnp.float32)
    gate_acts = jnp.where(own, gate_acts, 0.0)
    up_acts = jnp.where(own, up_acts, 0.0)
    sigmoid_g = jax.nn.sigmoid(gate_acts)
    silu_g = gate_acts * sigmoid_g
    hidden = (silu_g * up_acts).astype(jnp.bfloat16)
    out_halves = [
        jnp.einsum("srlh,lhd->srd", hidden, w, preferred_element_type=jnp.float32)
        for w in halves_of(w_down, 2)
    ]
    d_out, out_halves = lax.optimization_barrier((d_out, out_halves))
    got_out = send_back(out_halves)
    stacked = jnp.broadcast_to(
        jnp.stack([weight_hi, weight_lo]).reshape(2, tok_count, owners, 1, rows_per_owner),
        (2, tok_count, owners, cols, rows_per_owner),
    )
    both_parts = jnp.dot(
        stacked.reshape(2 * tok_count, owners * cols * rows_per_owner),
        flat(got_out),
        preferred_element_type=jnp.float32,
    )
    mixed = (both_parts[:tok_count] + both_parts[tok_count:]).astype(jnp.bfloat16)
    dots = lax.dot_general(
        cotangent, flat(got_out), (((1,), (1,)), ((), ())), preferred_element_type=jnp.float32
    ).reshape(tok_count, owners, cols, rows_per_owner)
    dots = jnp.sum(dots, axis=2).reshape(tok_count, 1, slots)
    prob_part = jnp.sum(jnp.where(match, dots, 0.0), axis=2)

    grad_down = jnp.einsum(
        "srlh,scrd->lhcd", hidden, d_out, preferred_element_type=jnp.float32
    ).astype(jnp.bfloat16).reshape(w_down.shape)
    d_hidden = jnp.einsum("scrd,lhcd->srlh", d_out, w_down_h, preferred_element_type=jnp.float32)
    d_hidden = jnp.where(own, d_hidden, 0.0)
    d_gate = (d_hidden * up_acts * sigmoid_g * (1.0 + gate_acts * (1.0 - sigmoid_g))).astype(
        jnp.bfloat16
    )
    d_up = (d_hidden * silu_g).astype(jnp.bfloat16)
    grad_gate = jnp.einsum(
        "scrd,srlh->lcdh", row_block, d_gate, preferred_element_type=jnp.float32
    ).astype(jnp.bfloat16).reshape(w_gate.shape)
    grad_up = jnp.einsum(
        "scrd,srlh->lcdh", row_block, d_up, preferred_element_type=jnp.float32
    ).astype(jnp.bfloat16).reshape(w_up.shape)
    got_grad = send_back(
        [
            jnp.einsum("srlh,ldh->srd", d_gate, wg, preferred_element_type=jnp.float32)
            + jnp.einsum("srlh,ldh->srd", d_up, wu, preferred_element_type=jnp.float32)
            for wg, wu in zip(halves_of(w_gate, 1), halves_of(w_up, 1))
        ]
    )
    grad_tokens = combine(picker, got_grad).astype(jnp.bfloat16)
    prob_part, mixed = lax.optimization_barrier((prob_part, mixed))
    grad_probs = lax.psum(prob_part, "col")
    return (mixed, grad_tokens, grad_probs, grad_gate, grad_up, grad_down)


def solution(mesh):
    return jax.shard_map(
        body,
        mesh=mesh,
        in_specs=(
            P("dp", None),
            P("dp", None),
            P("dp", None),
            P("dp", None, "col"),
            P("dp", None, "col"),
            P("dp", "col", None),
            P("dp", "col"),
        ),
        out_specs=(
            P("dp", "col"),
            P("dp", "col"),
            P("dp", None),
            P("dp", None, "col"),
            P("dp", None, "col"),
            P("dp", "col", None),
        ),
        check_vma=False,
    )
```

```python
import jax
import jax.numpy as jnp
from jax import lax
from jax.sharding import PartitionSpec as P


def body(tokens, routes, probs, w_gate, w_up, w_down, cotangent):
    tok_count, width = tokens.shape
    top_count = routes.shape[1]
    owners = lax.axis_size("dp")
    cols = lax.axis_size("col")
    local_experts = w_gate.shape[0]
    experts = local_experts * owners
    slot_cap = 3 * tok_count * top_count // (2 * experts)
    half_width = width // cols
    pair_count = tok_count * top_count
    rows_per_owner = local_experts * slot_cap
    slots = experts * slot_cap

    flat_routes = routes.reshape(-1)
    expert_ids = jnp.arange(experts, dtype=jnp.int32)
    onehot = (flat_routes[:, None] == expert_ids[None, :]).astype(jnp.int32)
    before = jnp.cumsum(onehot, axis=0) - onehot
    slot_index = jnp.sum(before * onehot, axis=1)
    flat_index = flat_routes * slot_cap + slot_index

    slot_ids = jnp.arange(slots, dtype=jnp.int32)
    match = flat_index.reshape(tok_count, top_count)[:, :, None] == slot_ids[None, None, :]
    weight = jnp.sum(jnp.where(match, probs[:, :, None], 0.0), axis=1)
    taken = jnp.any(match, axis=1)
    picker = taken.astype(jnp.bfloat16)
    weight_hi = weight.astype(jnp.bfloat16)
    weight_lo = (weight - weight_hi.astype(jnp.float32)).astype(jnp.bfloat16)
    prob_of_slot = jnp.sum(weight, axis=0)

    both = ("dp", "col")

    col_me = lax.axis_index("col")
    tok_half = lax.dynamic_slice_in_dim(tokens, col_me * half_width, half_width, axis=1)
    tok_rows = jnp.einsum("ts,td->sd", picker, tok_half, preferred_element_type=jnp.float32)
    cot_rows = jnp.einsum("ts,td->sd", picker, cotangent, preferred_element_type=jnp.float32)

    def spread(rows_half):
        return jnp.broadcast_to(
            rows_half.reshape(owners, 1, rows_per_owner, half_width),
            (owners, cols, rows_per_owner, half_width),
        ).reshape(owners * cols, rows_per_owner, half_width)

    def dispatch(sent):
        got = lax.all_to_all(sent, both, 0, 0, tiled=True)
        return got.reshape(owners, cols, rows_per_owner, half_width)

    tok_sent, cot_sent = lax.optimization_barrier(
        (
            spread(tok_rows.astype(jnp.bfloat16)),
            spread((prob_of_slot[:, None] * cot_rows).astype(jnp.bfloat16)),
        )
    )
    row_block = dispatch(tok_sent)
    d_out = dispatch(cot_sent)
    w_gate_h = w_gate.reshape(local_experts, cols, half_width, -1)
    w_up_h = w_up.reshape(local_experts, cols, half_width, -1)
    w_down_h = w_down.reshape(local_experts, w_down.shape[1], cols, half_width)

    expert_of_row = jnp.arange(rows_per_owner, dtype=jnp.int32) // slot_cap
    own = (expert_of_row[:, None] == jnp.arange(local_experts, dtype=jnp.int32)[None, :])[
        None, :, :, None
    ]

    def per_half(table):
        return jnp.broadcast_to(
            table.reshape(tok_count, owners, 1, rows_per_owner),
            (tok_count, owners, cols, rows_per_owner),
        )

    def send_back(halves):
        part = jnp.stack([h.astype(jnp.bfloat16) for h in halves], axis=1)
        got = lax.all_to_all(
            part.reshape(owners * cols, rows_per_owner, half_width), both, 0, 0, tiled=True
        )
        return got.reshape(owners, cols, rows_per_owner, half_width)

    def flat(got):
        return got.reshape(owners * cols * rows_per_owner, half_width)

    def combine(table, got):
        lhs = per_half(table).reshape(tok_count, owners * cols * rows_per_owner)
        return jnp.dot(lhs, flat(got), preferred_element_type=jnp.float32)

    def halves_of(ref, axis):
        return [lax.slice_in_dim(ref, j * half_width, (j + 1) * half_width, axis=axis) for j in range(cols)]

    gate_acts = jnp.einsum("scrd,lcdh->srlh", row_block, w_gate_h, preferred_element_type=jnp.float32)
    up_acts = jnp.einsum("scrd,lcdh->srlh", row_block, w_up_h, preferred_element_type=jnp.float32)
    gate_acts = jnp.where(own, gate_acts, 0.0)
    up_acts = jnp.where(own, up_acts, 0.0)
    sigmoid_g = jax.nn.sigmoid(gate_acts)
    silu_g = gate_acts * sigmoid_g
    hidden = (silu_g * up_acts).astype(jnp.bfloat16)
    out_halves = [
        jnp.einsum("srlh,lhd->srd", hidden, w, preferred_element_type=jnp.float32)
        for w in halves_of(w_down, 2)
    ]
    d_out, out_halves = lax.optimization_barrier((d_out, out_halves))
    got_out = send_back(out_halves)
    stacked = jnp.broadcast_to(
        jnp.stack([weight_hi, weight_lo]).reshape(2, tok_count, owners, 1, rows_per_owner),
        (2, tok_count, owners, cols, rows_per_owner),
    )
    both_parts = jnp.dot(
        stacked.reshape(2 * tok_count, owners * cols * rows_per_owner),
        flat(got_out),
        preferred_element_type=jnp.float32,
    )
    mixed = (both_parts[:tok_count] + both_parts[tok_count:]).astype(jnp.bfloat16)
    dots = lax.dot_general(
        cotangent, flat(got_out), (((1,), (1,)), ((), ())), preferred_element_type=jnp.float32
    ).reshape(tok_count, owners, cols, rows_per_owner)
    dots = jnp.sum(dots, axis=2).reshape(tok_count, 1, slots)
    prob_part = jnp.sum(jnp.where(match, dots, 0.0), axis=2)

    grad_down = jnp.einsum(
        "srlh,scrd->lhcd", hidden, d_out, preferred_element_type=jnp.float32
    ).astype(jnp.bfloat16).reshape(w_down.shape)
    d_hidden = jnp.einsum("scrd,lhcd->srlh", d_out, w_down_h, preferred_element_type=jnp.float32)
    d_hidden = jnp.where(own, d_hidden, 0.0)
    d_gate = (d_hidden * up_acts * sigmoid_g * (1.0 + gate_acts * (1.0 - sigmoid_g))).astype(
        jnp.bfloat16
    )
    d_up = (d_hidden * silu_g).astype(jnp.bfloat16)
    grad_gate = jnp.einsum(
        "scrd,srlh->lcdh", row_block, d_gate, preferred_element_type=jnp.float32
    ).astype(jnp.bfloat16).reshape(w_gate.shape)
    grad_up = jnp.einsum(
        "scrd,srlh->lcdh", row_block, d_up, preferred_element_type=jnp.float32
    ).astype(jnp.bfloat16).reshape(w_up.shape)
    got_grad = send_back(
        [
            jnp.einsum("srlh,ldh->srd", d_gate, wg, preferred_element_type=jnp.float32)
            + jnp.einsum("srlh,ldh->srd", d_up, wu, preferred_element_type=jnp.float32)
            for wg, wu in zip(halves_of(w_gate, 1), halves_of(w_up, 1))
        ]
    )
    grad_tokens = combine(picker, got_grad).astype(jnp.bfloat16)
    prob_part, mixed = lax.optimization_barrier((prob_part, mixed))
    grad_probs = lax.psum(prob_part, "col")
    return (mixed, grad_tokens, grad_probs, grad_gate, grad_up, grad_down)


def solution(mesh):
    return jax.shard_map(
        body,
        mesh=mesh,
        in_specs=(
            P("dp", None),
            P("dp", None),
            P("dp", None),
            P("dp", None, "col"),
            P("dp", None, "col"),
            P("dp", "col", None),
            P("dp", "col"),
        ),
        out_specs=(
            P("dp", "col"),
            P("dp", "col"),
            P("dp", None),
            P("dp", None, "col"),
            P("dp", None, "col"),
            P("dp", "col", None),
        ),
        check_vma=False,
    )
```

```python
import jax
import jax.numpy as jnp
from jax import lax
from jax.sharding import PartitionSpec as P


def body(tokens, routes, probs, w_gate, w_up, w_down, cotangent):
    tok_count, width = tokens.shape
    top_count = routes.shape[1]
    owners = lax.axis_size("dp")
    cols = lax.axis_size("col")
    local_experts = w_gate.shape[0]
    experts = local_experts * owners
    slot_cap = 3 * tok_count * top_count // (2 * experts)
    half_width = width // cols
    pair_count = tok_count * top_count
    rows_per_owner = local_experts * slot_cap
    slots = experts * slot_cap

    flat_routes = routes.reshape(-1)
    expert_ids = jnp.arange(experts, dtype=jnp.int32)
    onehot = (flat_routes[:, None] == expert_ids[None, :]).astype(jnp.int32)
    before = jnp.cumsum(onehot, axis=0) - onehot
    slot_index = jnp.sum(before * onehot, axis=1)
    flat_index = flat_routes * slot_cap + slot_index

    slot_ids = jnp.arange(slots, dtype=jnp.int32)
    match = flat_index.reshape(tok_count, top_count)[:, :, None] == slot_ids[None, None, :]
    weight = jnp.sum(jnp.where(match, probs[:, :, None], 0.0), axis=1)
    taken = jnp.any(match, axis=1)
    picker = taken.astype(jnp.bfloat16)
    weight_hi = weight.astype(jnp.bfloat16)
    weight_lo = (weight - weight_hi.astype(jnp.float32)).astype(jnp.bfloat16)
    prob_of_slot = jnp.sum(weight, axis=0)

    both = ("dp", "col")

    col_me = lax.axis_index("col")
    tok_half = lax.dynamic_slice_in_dim(tokens, col_me * half_width, half_width, axis=1)
    tok_rows = jnp.einsum("ts,td->sd", picker, tok_half, preferred_element_type=jnp.float32)
    cot_rows = jnp.einsum("ts,td->sd", picker, cotangent, preferred_element_type=jnp.float32)

    def spread(rows_half):
        return jnp.broadcast_to(
            rows_half.reshape(owners, 1, rows_per_owner, half_width),
            (owners, cols, rows_per_owner, half_width),
        ).reshape(owners * cols, rows_per_owner, half_width)

    def dispatch(sent):
        got = lax.all_to_all(sent, both, 0, 0, tiled=True)
        return got.reshape(owners, cols, rows_per_owner, half_width)

    tok_sent, cot_sent = lax.optimization_barrier(
        (
            spread(tok_rows.astype(jnp.bfloat16)),
            spread((prob_of_slot[:, None] * cot_rows).astype(jnp.bfloat16)),
        )
    )
    row_block = dispatch(tok_sent)
    d_out = dispatch(cot_sent)
    w_gate_h = w_gate.reshape(local_experts, cols, half_width, -1)
    w_up_h = w_up.reshape(local_experts, cols, half_width, -1)
    w_down_h = w_down.reshape(local_experts, w_down.shape[1], cols, half_width)

    expert_of_row = jnp.arange(rows_per_owner, dtype=jnp.int32) // slot_cap
    own = (expert_of_row[:, None] == jnp.arange(local_experts, dtype=jnp.int32)[None, :])[
        None, :, :, None
    ]

    def per_half(table):
        return jnp.broadcast_to(
            table.reshape(tok_count, owners, 1, rows_per_owner),
            (tok_count, owners, cols, rows_per_owner),
        )

    def pack(halves):
        return jnp.stack([h.astype(jnp.bfloat16) for h in halves], axis=1)

    def send_back(part):
        got = lax.all_to_all(
            part.reshape(owners * cols, rows_per_owner, half_width), both, 0, 0, tiled=True
        )
        return got.reshape(owners, cols, rows_per_owner, half_width)

    def flat(got):
        return got.reshape(owners * cols * rows_per_owner, half_width)

    def combine(table, got):
        lhs = per_half(table).reshape(tok_count, owners * cols * rows_per_owner)
        return jnp.dot(lhs, flat(got), preferred_element_type=jnp.float32)

    def halves_of(ref, axis):
        return [lax.slice_in_dim(ref, j * half_width, (j + 1) * half_width, axis=axis) for j in range(cols)]

    gate_acts = jnp.einsum("scrd,lcdh->srlh", row_block, w_gate_h, preferred_element_type=jnp.float32)
    up_acts = jnp.einsum("scrd,lcdh->srlh", row_block, w_up_h, preferred_element_type=jnp.float32)
    gate_acts = jnp.where(own, gate_acts, 0.0)
    up_acts = jnp.where(own, up_acts, 0.0)
    sigmoid_g = jax.nn.sigmoid(gate_acts)
    silu_g = gate_acts * sigmoid_g
    hidden = (silu_g * up_acts).astype(jnp.bfloat16)
    out_halves = [
        jnp.einsum("srlh,lhd->srd", hidden, w, preferred_element_type=jnp.float32)
        for w in halves_of(w_down, 2)
    ]
    out_part = pack(out_halves)
    d_out, out_part = lax.optimization_barrier((d_out, out_part))
    got_out = send_back(out_part)
    stacked = jnp.broadcast_to(
        jnp.stack([weight_hi, weight_lo]).reshape(2, tok_count, owners, 1, rows_per_owner),
        (2, tok_count, owners, cols, rows_per_owner),
    )
    both_parts = jnp.dot(
        stacked.reshape(2 * tok_count, owners * cols * rows_per_owner),
        flat(got_out),
        preferred_element_type=jnp.float32,
    )
    mixed = (both_parts[:tok_count] + both_parts[tok_count:]).astype(jnp.bfloat16)
    dots = lax.dot_general(
        cotangent, flat(got_out), (((1,), (1,)), ((), ())), preferred_element_type=jnp.float32
    ).reshape(tok_count, owners, cols, rows_per_owner)
    dots = jnp.sum(dots, axis=2).reshape(tok_count, 1, slots)
    prob_part = jnp.sum(jnp.where(match, dots, 0.0), axis=2)

    grad_down = jnp.einsum(
        "srlh,scrd->lhcd", hidden, d_out, preferred_element_type=jnp.float32
    ).astype(jnp.bfloat16).reshape(w_down.shape)
    d_hidden = jnp.einsum("scrd,lhcd->srlh", d_out, w_down_h, preferred_element_type=jnp.float32)
    d_hidden = jnp.where(own, d_hidden, 0.0)
    d_gate = (d_hidden * up_acts * sigmoid_g * (1.0 + gate_acts * (1.0 - sigmoid_g))).astype(
        jnp.bfloat16
    )
    d_up = (d_hidden * silu_g).astype(jnp.bfloat16)
    grad_gate = jnp.einsum(
        "scrd,srlh->lcdh", row_block, d_gate, preferred_element_type=jnp.float32
    ).astype(jnp.bfloat16).reshape(w_gate.shape)
    grad_up = jnp.einsum(
        "scrd,srlh->lcdh", row_block, d_up, preferred_element_type=jnp.float32
    ).astype(jnp.bfloat16).reshape(w_up.shape)
    got_grad = send_back(pack(
        [
            jnp.einsum("srlh,ldh->srd", d_gate, wg, preferred_element_type=jnp.float32)
            + jnp.einsum("srlh,ldh->srd", d_up, wu, preferred_element_type=jnp.float32)
            for wg, wu in zip(halves_of(w_gate, 1), halves_of(w_up, 1))
        ]
    ))
    grad_tokens = combine(picker, got_grad).astype(jnp.bfloat16)
    prob_part, mixed = lax.optimization_barrier((prob_part, mixed))
    grad_probs = lax.psum(prob_part, "col")
    return (mixed, grad_tokens, grad_probs, grad_gate, grad_up, grad_down)


def solution(mesh):
    return jax.shard_map(
        body,
        mesh=mesh,
        in_specs=(
            P("dp", None),
            P("dp", None),
            P("dp", None),
            P("dp", None, "col"),
            P("dp", None, "col"),
            P("dp", "col", None),
            P("dp", "col"),
        ),
        out_specs=(
            P("dp", "col"),
            P("dp", "col"),
            P("dp", None),
            P("dp", None, "col"),
            P("dp", None, "col"),
            P("dp", "col", None),
        ),
        check_vma=False,
    )
```

```python
import jax
import jax.numpy as jnp
from jax import lax
from jax.sharding import PartitionSpec as P


def body(tokens, routes, probs, w_gate, w_up, w_down, cotangent):
    tok_count, width = tokens.shape
    top_count = routes.shape[1]
    owners = lax.axis_size("dp")
    cols = lax.axis_size("col")
    local_experts = w_gate.shape[0]
    experts = local_experts * owners
    slot_cap = 3 * tok_count * top_count // (2 * experts)
    half_width = width // cols
    pair_count = tok_count * top_count
    rows_per_owner = local_experts * slot_cap
    slots = experts * slot_cap

    flat_routes = routes.reshape(-1)
    expert_ids = jnp.arange(experts, dtype=jnp.int32)
    onehot = (flat_routes[:, None] == expert_ids[None, :]).astype(jnp.int32)
    before = jnp.cumsum(onehot, axis=0) - onehot
    slot_index = jnp.sum(before * onehot, axis=1)
    flat_index = flat_routes * slot_cap + slot_index

    slot_ids = jnp.arange(slots, dtype=jnp.int32)
    match = flat_index.reshape(tok_count, top_count)[:, :, None] == slot_ids[None, None, :]
    weight = jnp.sum(jnp.where(match, probs[:, :, None], 0.0), axis=1)
    taken = jnp.any(match, axis=1)
    picker = taken.astype(jnp.bfloat16)
    weight_hi = weight.astype(jnp.bfloat16)
    weight_lo = (weight - weight_hi.astype(jnp.float32)).astype(jnp.bfloat16)
    prob_of_slot = jnp.sum(weight, axis=0)

    both = ("dp", "col")

    col_me = lax.axis_index("col")
    tok_half = lax.dynamic_slice_in_dim(tokens, col_me * half_width, half_width, axis=1)
    tok_rows = jnp.einsum("ts,td->sd", picker, tok_half, preferred_element_type=jnp.float32)
    cot_rows = jnp.einsum("ts,td->sd", picker, cotangent, preferred_element_type=jnp.float32)

    def spread(rows_half):
        return jnp.broadcast_to(
            rows_half.reshape(owners, 1, rows_per_owner, half_width),
            (owners, cols, rows_per_owner, half_width),
        ).reshape(owners * cols, rows_per_owner, half_width)

    def dispatch(sent):
        got = lax.all_to_all(sent, both, 0, 0, tiled=True)
        return got.reshape(owners, cols, rows_per_owner, half_width)

    tok_sent, cot_sent = lax.optimization_barrier(
        (
            spread(tok_rows.astype(jnp.bfloat16)),
            spread((prob_of_slot[:, None] * cot_rows).astype(jnp.bfloat16)),
        )
    )
    row_block = dispatch(tok_sent)
    d_out = dispatch(cot_sent)
    w_gate_h = w_gate.reshape(local_experts, cols, half_width, -1)
    w_up_h = w_up.reshape(local_experts, cols, half_width, -1)
    w_down_h = w_down.reshape(local_experts, w_down.shape[1], cols, half_width)

    expert_of_row = jnp.arange(rows_per_owner, dtype=jnp.int32) // slot_cap
    own = (expert_of_row[:, None] == jnp.arange(local_experts, dtype=jnp.int32)[None, :])[
        None, :, :, None
    ]

    def per_half(table):
        return jnp.broadcast_to(
            table.reshape(tok_count, owners, 1, rows_per_owner),
            (tok_count, owners, cols, rows_per_owner),
        )

    def send_back(part):
        part = part.astype(jnp.bfloat16)
        got = lax.all_to_all(
            part.reshape(owners * cols, rows_per_owner, half_width), both, 0, 0, tiled=True
        )
        return got.reshape(owners, cols, rows_per_owner, half_width)

    def flat(got):
        return got.reshape(owners * cols * rows_per_owner, half_width)

    def combine(table, got):
        lhs = per_half(table).reshape(tok_count, owners * cols * rows_per_owner)
        return jnp.dot(lhs, flat(got), preferred_element_type=jnp.float32)

    def halves_of(ref, axis):
        return [lax.slice_in_dim(ref, j * half_width, (j + 1) * half_width, axis=axis) for j in range(cols)]

    gate_acts = jnp.einsum("scrd,lcdh->srlh", row_block, w_gate_h, preferred_element_type=jnp.float32)
    up_acts = jnp.einsum("scrd,lcdh->srlh", row_block, w_up_h, preferred_element_type=jnp.float32)
    gate_acts = jnp.where(own, gate_acts, 0.0)
    up_acts = jnp.where(own, up_acts, 0.0)
    sigmoid_g = jax.nn.sigmoid(gate_acts)
    silu_g = gate_acts * sigmoid_g
    hidden = (silu_g * up_acts).astype(jnp.bfloat16)
    out_halves = jnp.einsum("srlh,lhjd->sjrd", hidden, w_down_h, preferred_element_type=jnp.float32)
    d_out, out_halves = lax.optimization_barrier((d_out, out_halves))
    got_out = send_back(out_halves)
    stacked = jnp.broadcast_to(
        jnp.stack([weight_hi, weight_lo]).reshape(2, tok_count, owners, 1, rows_per_owner),
        (2, tok_count, owners, cols, rows_per_owner),
    )
    both_parts = jnp.dot(
        stacked.reshape(2 * tok_count, owners * cols * rows_per_owner),
        flat(got_out),
        preferred_element_type=jnp.float32,
    )
    mixed = (both_parts[:tok_count] + both_parts[tok_count:]).astype(jnp.bfloat16)
    dots = lax.dot_general(
        cotangent, flat(got_out), (((1,), (1,)), ((), ())), preferred_element_type=jnp.float32
    ).reshape(tok_count, owners, cols, rows_per_owner)
    dots = jnp.sum(dots, axis=2).reshape(tok_count, 1, slots)
    prob_part = jnp.sum(jnp.where(match, dots, 0.0), axis=2)

    grad_down = jnp.einsum(
        "srlh,scrd->lhcd", hidden, d_out, preferred_element_type=jnp.float32
    ).astype(jnp.bfloat16).reshape(w_down.shape)
    d_hidden = jnp.einsum("scrd,lhcd->srlh", d_out, w_down_h, preferred_element_type=jnp.float32)
    d_hidden = jnp.where(own, d_hidden, 0.0)
    d_gate = (d_hidden * up_acts * sigmoid_g * (1.0 + gate_acts * (1.0 - sigmoid_g))).astype(
        jnp.bfloat16
    )
    d_up = (d_hidden * silu_g).astype(jnp.bfloat16)
    grad_gate = jnp.einsum(
        "scrd,srlh->lcdh", row_block, d_gate, preferred_element_type=jnp.float32
    ).astype(jnp.bfloat16).reshape(w_gate.shape)
    grad_up = jnp.einsum(
        "scrd,srlh->lcdh", row_block, d_up, preferred_element_type=jnp.float32
    ).astype(jnp.bfloat16).reshape(w_up.shape)
    got_grad = send_back(
        jnp.einsum("srlh,ljdh->sjrd", d_gate, w_gate_h, preferred_element_type=jnp.float32)
        + jnp.einsum("srlh,ljdh->sjrd", d_up, w_up_h, preferred_element_type=jnp.float32)
    )
    grad_tokens = combine(picker, got_grad).astype(jnp.bfloat16)
    prob_part, mixed = lax.optimization_barrier((prob_part, mixed))
    grad_probs = lax.psum(prob_part, "col")
    return (mixed, grad_tokens, grad_probs, grad_gate, grad_up, grad_down)


def solution(mesh):
    return jax.shard_map(
        body,
        mesh=mesh,
        in_specs=(
            P("dp", None),
            P("dp", None),
            P("dp", None),
            P("dp", None, "col"),
            P("dp", None, "col"),
            P("dp", "col", None),
            P("dp", "col"),
        ),
        out_specs=(
            P("dp", "col"),
            P("dp", "col"),
            P("dp", None),
            P("dp", None, "col"),
            P("dp", None, "col"),
            P("dp", "col", None),
        ),
        check_vma=False,
    )
```

```python
import jax
import jax.numpy as jnp
from jax import lax
from jax.sharding import PartitionSpec as P


def body(tokens, routes, probs, w_gate, w_up, w_down, cotangent):
    tok_count, width = tokens.shape
    top_count = routes.shape[1]
    owners = lax.axis_size("dp")
    cols = lax.axis_size("col")
    local_experts = w_gate.shape[0]
    experts = local_experts * owners
    slot_cap = 3 * tok_count * top_count // (2 * experts)
    half_width = width // cols
    pair_count = tok_count * top_count
    rows_per_owner = local_experts * slot_cap
    slots = experts * slot_cap

    flat_routes = routes.reshape(-1)
    expert_ids = jnp.arange(experts, dtype=jnp.int32)
    onehot = (flat_routes[:, None] == expert_ids[None, :]).astype(jnp.int32)
    before = jnp.cumsum(onehot, axis=0) - onehot
    slot_index = jnp.sum(before * onehot, axis=1)
    flat_index = flat_routes * slot_cap + slot_index

    slot_ids = jnp.arange(slots, dtype=jnp.int32)
    match = flat_index.reshape(tok_count, top_count)[:, :, None] == slot_ids[None, None, :]
    weight = jnp.sum(jnp.where(match, probs[:, :, None], 0.0), axis=1)
    taken = jnp.any(match, axis=1)
    picker = taken.astype(jnp.bfloat16)
    weight_hi = weight.astype(jnp.bfloat16)
    weight_lo = (weight - weight_hi.astype(jnp.float32)).astype(jnp.bfloat16)
    prob_of_slot = jnp.sum(weight, axis=0)

    both = ("dp", "col")

    col_me = lax.axis_index("col")
    tok_half = lax.dynamic_slice_in_dim(tokens, col_me * half_width, half_width, axis=1)
    tok_rows = jnp.einsum("ts,td->sd", picker, tok_half, preferred_element_type=jnp.float32)
    cot_rows = jnp.einsum("ts,td->sd", picker, cotangent, preferred_element_type=jnp.float32)

    def spread(rows_half):
        return jnp.broadcast_to(
            rows_half.reshape(owners, 1, rows_per_owner, half_width),
            (owners, cols, rows_per_owner, half_width),
        ).reshape(owners * cols, rows_per_owner, half_width)

    def dispatch(sent):
        got = lax.all_to_all(sent, both, 0, 0, tiled=True)
        return got.reshape(owners, cols, rows_per_owner, half_width)

    tok_sent, cot_sent = lax.optimization_barrier(
        (
            spread(tok_rows.astype(jnp.bfloat16)),
            spread((prob_of_slot[:, None] * cot_rows).astype(jnp.bfloat16)),
        )
    )
    row_block = dispatch(tok_sent)
    d_out = dispatch(cot_sent)
    w_gate_h = w_gate.reshape(local_experts, cols, half_width, -1)
    w_up_h = w_up.reshape(local_experts, cols, half_width, -1)
    w_down_h = w_down.reshape(local_experts, w_down.shape[1], cols, half_width)

    expert_of_row = jnp.arange(rows_per_owner, dtype=jnp.int32) // slot_cap
    own = (expert_of_row[:, None] == jnp.arange(local_experts, dtype=jnp.int32)[None, :])[
        None, :, :, None
    ]

    def per_half(table):
        return jnp.broadcast_to(
            table.reshape(tok_count, owners, 1, rows_per_owner),
            (tok_count, owners, cols, rows_per_owner),
        )

    def send_back(halves):
        if isinstance(halves, list):
            halves = jnp.stack(halves, axis=1)
        part = halves.astype(jnp.bfloat16)
        got = lax.all_to_all(
            part.reshape(owners * cols, rows_per_owner, half_width), both, 0, 0, tiled=True
        )
        return got.reshape(owners, cols, rows_per_owner, half_width)

    def flat(got):
        return got.reshape(owners * cols * rows_per_owner, half_width)

    def combine(table, got):
        lhs = per_half(table).reshape(tok_count, owners * cols * rows_per_owner)
        return jnp.dot(lhs, flat(got), preferred_element_type=jnp.float32)

    def halves_of(ref, axis):
        return [lax.slice_in_dim(ref, j * half_width, (j + 1) * half_width, axis=axis) for j in range(cols)]

    gate_acts = jnp.einsum("scrd,lcdh->srlh", row_block, w_gate_h, preferred_element_type=jnp.float32)
    up_acts = jnp.einsum("scrd,lcdh->srlh", row_block, w_up_h, preferred_element_type=jnp.float32)
    gate_acts = jnp.where(own, gate_acts, 0.0)
    up_acts = jnp.where(own, up_acts, 0.0)
    sigmoid_g = jax.nn.sigmoid(gate_acts)
    silu_g = gate_acts * sigmoid_g
    hidden = (silu_g * up_acts).astype(jnp.bfloat16)
    out_halves = [
        jnp.einsum("srlh,lhd->srd", hidden, w, preferred_element_type=jnp.float32)
        for w in halves_of(w_down, 2)
    ]
    d_out, out_halves = lax.optimization_barrier((d_out, out_halves))
    got_out = send_back(out_halves)
    stacked = jnp.broadcast_to(
        jnp.stack([weight_hi, weight_lo]).reshape(2, tok_count, owners, 1, rows_per_owner),
        (2, tok_count, owners, cols, rows_per_owner),
    )
    both_parts = jnp.dot(
        stacked.reshape(2 * tok_count, owners * cols * rows_per_owner),
        flat(got_out),
        preferred_element_type=jnp.float32,
    )
    mixed = (both_parts[:tok_count] + both_parts[tok_count:]).astype(jnp.bfloat16)
    dots = lax.dot_general(
        cotangent, flat(got_out), (((1,), (1,)), ((), ())), preferred_element_type=jnp.float32
    ).reshape(tok_count, owners, cols, rows_per_owner)
    dots = jnp.sum(dots, axis=2).reshape(tok_count, 1, slots)
    prob_part = jnp.sum(jnp.where(match, dots, 0.0), axis=2)

    grad_down = jnp.einsum(
        "srlh,scrd->lhcd", hidden, d_out, preferred_element_type=jnp.float32
    ).astype(jnp.bfloat16).reshape(w_down.shape)
    d_hidden = jnp.einsum("scrd,lhcd->srlh", d_out, w_down_h, preferred_element_type=jnp.float32)
    d_hidden = jnp.where(own, d_hidden, 0.0)
    d_gate = (d_hidden * up_acts * sigmoid_g * (1.0 + gate_acts * (1.0 - sigmoid_g))).astype(
        jnp.bfloat16
    )
    d_up = (d_hidden * silu_g).astype(jnp.bfloat16)
    grad_gate = jnp.einsum(
        "scrd,srlh->lcdh", row_block, d_gate, preferred_element_type=jnp.float32
    ).astype(jnp.bfloat16).reshape(w_gate.shape)
    grad_up = jnp.einsum(
        "scrd,srlh->lcdh", row_block, d_up, preferred_element_type=jnp.float32
    ).astype(jnp.bfloat16).reshape(w_up.shape)
    got_grad = send_back(
        jnp.einsum("srlh,ljdh->sjrd", d_gate, w_gate_h, preferred_element_type=jnp.float32)
        + jnp.einsum("srlh,ljdh->sjrd", d_up, w_up_h, preferred_element_type=jnp.float32)
    )
    grad_tokens = combine(picker, got_grad).astype(jnp.bfloat16)
    prob_part, mixed = lax.optimization_barrier((prob_part, mixed))
    grad_probs = lax.psum(prob_part, "col")
    return (mixed, grad_tokens, grad_probs, grad_gate, grad_up, grad_down)


def solution(mesh):
    return jax.shard_map(
        body,
        mesh=mesh,
        in_specs=(
            P("dp", None),
            P("dp", None),
            P("dp", None),
            P("dp", None, "col"),
            P("dp", None, "col"),
            P("dp", "col", None),
            P("dp", "col"),
        ),
        out_specs=(
            P("dp", "col"),
            P("dp", "col"),
            P("dp", None),
            P("dp", None, "col"),
            P("dp", None, "col"),
            P("dp", "col", None),
        ),
        check_vma=False,
    )
```
